32 devices in a mesh: dp: 2 (over x), blk: 4 (over y, core), ulysses: 4 (over z).
Axes of the slice: x: 2, y: 2, z: 4, core: 2. Of those that a mesh axis runs over, the one named last changes fastest.
Arguments:
- tokens: bfloat16 [2, 2048, 1024], P('dp', ('blk', 'ulysses')), may hold values from -20 to 20
- query_weight: bfloat16 [1024, 1024], P(('dp', 'blk'), 'ulysses')
- key_weight: bfloat16 [1024, 1024], P(('dp', 'blk'), 'ulysses')
- value_weight: bfloat16 [1024, 1024], P(('dp', 'blk'), 'ulysses'), may hold values from -0.1875 to 0.1875
- out_weight: bfloat16 [1024, 1024], P('ulysses', ('dp', 'blk'))
- query_bias: bfloat16 [16, 64], P('ulysses', ('dp', 'blk')), may hold values from -4 to 4
- value_bias: bfloat16 [16, 64], P('ulysses', ('dp', 'blk'))
- out_bias: bfloat16 [1024], P(('dp', 'blk')), may hold values from -4 to 4
- norm1_gain: bfloat16 [1024], P(('dp', 'blk')), may hold values from 0.5 to 1.5
- norm1_shift: bfloat16 [1024], P(('dp', 'blk')), may hold values from -4 to 4
- inner_weight: bfloat16 [1024, 4096], P(('dp', 'blk'), 'ulysses'), may hold values from -0.1875 to 0.1875
- inner_bias: bfloat16 [64, 64], P('ulysses', ('dp', 'blk')), may hold values from -4 to 4
- outer_weight: bfloat16 [4096, 1024], P('ulysses', ('dp', 'blk')), may hold values from -0.09375 to 0.09375
- outer_bias: bfloat16 [1024], P(('dp', 'blk')), may hold values from -4 to 4
- norm2_gain: bfloat16 [1024], P(('dp', 'blk')), may hold values from 0.5 to 1.5
- norm2_shift: bfloat16 [1024], P(('dp', 'blk')), may hold values from -4 to 4
- out_grad: bfloat16 [2, 2048, 1024], P('dp', ('blk', 'ulysses')), may hold values from -6 to 6
Outputs:
- block_out: bfloat16 [2, 2048, 1024], P('dp', ('blk', 'ulysses'))
- tokens_grad: bfloat16 [2, 2048, 1024], P('dp', ('blk', 'ulysses'))
- query_weight_grad: float32 [1024, 1024], P(('dp', 'blk'), 'ulysses')
- key_weight_grad: float32 [1024, 1024], P(('dp', 'blk'), 'ulysses')
- value_weight_grad: float32 [1024, 1024], P(('dp', 'blk'), 'ulysses')
- out_weight_grad: float32 [1024, 1024], P('ulysses', ('dp', 'blk'))
- query_bias_grad: float32 [16, 64], P('ulysses', ('dp', 'blk'))
- value_bias_grad: float32 [16, 64], P('ulysses', ('dp', 'blk'))
- out_bias_grad: float32 [1024], P(('dp', 'blk'))
- norm1_gain_grad: float32 [1024], P(('dp', 'blk'))
- norm1_shift_grad: float32 [1024], P(('dp', 'blk'))
- inner_weight_grad: float32 [1024, 4096], P(('dp', 'blk'), 'ulysses')
- inner_bias_grad: float32 [64, 64], P('ulysses', ('dp', 'blk'))
- outer_weight_grad: float32 [4096, 1024], P('ulysses', ('dp', 'blk'))
- outer_bias_grad: float32 [1024], P(('dp', 'blk'))
- norm2_gain_grad: float32 [1024], P(('dp', 'blk'))
- norm2_shift_grad: float32 [1024], P(('dp', 'blk'))
The draws below stay inside these ranges and needn't reach their ends.
All inputs are finite; a program needn't handle non-finite values.
Results may differ from the reference program's by a relative error of at most 0.035.
Values may be sent and summed in bfloat16 or wider, within the bound.
A program may use at most 128 MiB of HBM per device.

```python
import math
import jax
import jax.numpy as jnp
from jax import lax

D = 1024
H = 16
DH = 64
FF = 4096
SEQ_LEN = 2048
SEQS = 2


def draw_tokens(key, part):
    shape = (SEQS, SEQ_LEN, D)
    first = jax.random.fold_in(key, 201)
    return jnp.clip(jax.random.normal(first, shape, jnp.float32), -6.0, 6.0).astype(jnp.bfloat16)


def paired_weights(key):
    first = jnp.clip(jax.random.normal(jax.random.fold_in(key, 101), (D, D), jnp.float32), -5.0, 5.0) * D ** (-0.5)
    other = jnp.clip(jax.random.normal(jax.random.fold_in(key, 102), (D, D), jnp.float32), -5.0, 5.0) * D ** (-0.5)
    return (first, other)


def draw_query_weight(key, part):
    return paired_weights(key)[0].astype(jnp.bfloat16)


def draw_key_weight(key, part):
    return paired_weights(key)[1].astype(jnp.bfloat16)


def draw_out_weight(key, part):
    factor = (SEQ_LEN / (2.7 * D)) ** 0.5
    return (jnp.clip(jax.random.normal(jax.random.fold_in(key, 301), (D, D), jnp.float32), -5.0, 5.0) * factor).astype(jnp.bfloat16)


def draw_value_bias(key, part):
    factor = 0.5 * (2.7 / SEQ_LEN) ** 0.5
    return (jnp.clip(jax.random.normal(jax.random.fold_in(key, 401), (H, DH), jnp.float32), -5.0, 5.0) * factor).astype(jnp.bfloat16)


def level_of(stream_key, dims, split, smallest, largest):
    def one(position, blocks):
        heights = jax.random.uniform(jax.random.fold_in(jax.random.fold_in(stream_key, 6), position), (blocks,), jnp.float32, smallest / len(split), largest / len(split))
        return jnp.repeat(jnp.exp(heights), dims[position] // blocks).reshape((-1,) + (1,) * (len(dims) - position - 1))

    loudness = one(*split[0])
    for cut in split[1:]:
        loudness = loudness * one(*cut)
    return loudness


def bell_draw(rng, extent, deviation, most, shards=(), kind=jnp.bfloat16):
    entries = jax.random.normal(rng, extent, jnp.float32) * deviation
    if len(shards) > 0:
        entries = level_of(rng, extent, shards, -0.22, 0.18) * entries
    return jnp.clip(entries, min=-most, max=most).astype(kind)


def setup_inputs(seed: int = 0) -> dict:
    streams_of = jax.random.split(jax.random.key(seed), 18)
    return {
        "tokens": draw_tokens(jax.random.fold_in(streams_of[17], 71), 0),
        "query_weight": draw_query_weight(jax.random.fold_in(streams_of[17], 71), 0),
        "key_weight": draw_key_weight(jax.random.fold_in(streams_of[17], 71), 0),
        "value_weight": bell_draw(streams_of[3], (D, D), D ** -0.5, 0.1875, ((0, 8), (1, 4))),
        "out_weight": draw_out_weight(jax.random.fold_in(streams_of[17], 71), 0),
        "query_bias": bell_draw(streams_of[5], (H, DH), 0.3, 4.0, ((0, 4), (1, 8))),
        "value_bias": draw_value_bias(jax.random.fold_in(streams_of[17], 71), 0),
        "out_bias": bell_draw(streams_of[7], (D,), 0.3, 4.0, ((0, 8),)),
        "norm1_gain": jnp.clip(1.0 + 0.1 * jax.random.normal(streams_of[8], (D,), jnp.float32), 0.5, 1.5).astype(jnp.bfloat16),
        "norm1_shift": bell_draw(streams_of[9], (D,), 0.3, 4.0, ((0, 8),)),
        "inner_weight": bell_draw(streams_of[10], (D, FF), D ** -0.5, 0.1875, ((0, 8), (1, 4))),
        "inner_bias": bell_draw(streams_of[11], (FF // DH, DH), 0.3, 4.0, ((0, 4), (1, 8))),
        "outer_weight": bell_draw(streams_of[12], (FF, D), FF ** -0.5, 0.09375, ((0, 4), (1, 8))),
        "outer_bias": bell_draw(streams_of[13], (D,), 0.3, 4.0, ((0, 8),)),
        "norm2_gain": jnp.clip(1.0 + 0.1 * jax.random.normal(streams_of[14], (D,), jnp.float32), 0.5, 1.5).astype(jnp.bfloat16),
        "norm2_shift": bell_draw(streams_of[15], (D,), 0.3, 4.0, ((0, 8),)),
        "out_grad": bell_draw(streams_of[16], (SEQS, SEQ_LEN, D), 1.0, 6.0, ((0, 2), (1, 16))),
    }


EPSILON = 1e-05

def gelu_parts(pre):
    cdf = 0.5 * (1.0 + lax.erf(pre * 0.7071067811865476))
    dens = jnp.exp(-0.5 * pre * pre) * 0.3989422804014327
    return (pre * cdf, cdf + pre * dens)

def norm_forward(resid, gain, shift):
    centre = resid - lax.optimization_barrier(jnp.mean(resid, axis=-1, keepdims=True))
    rstd = lax.rsqrt(lax.optimization_barrier(jnp.mean(centre * centre, axis=-1, keepdims=True)) + EPSILON)
    unit = centre * rstd
    return (unit * gain + shift, unit, rstd)

def norm_backward(grad, unit, rstd, gain):
    scaled = grad * gain
    inner = scaled - lax.optimization_barrier(jnp.mean(scaled, axis=-1, keepdims=True)) - unit * lax.optimization_barrier(jnp.mean(scaled * unit, axis=-1, keepdims=True))
    return (rstd * inner, lax.optimization_barrier(jnp.sum(grad * unit, axis=0)), lax.optimization_barrier(jnp.sum(grad, axis=0)))

def split_heads(rows):
    return rows.reshape(rows.shape[0], H, DH).transpose(1, 0, 2)

def merge_heads(rows):
    return rows.transpose(1, 0, 2).reshape(rows.shape[1], H * DH)

def attend(query, keys, values):
    length = query.shape[0]
    block = math.gcd(length, 512)
    count = length // block
    scale = DH ** (-0.5)

    def per_head(parts):
        q_head, k_head, v_head = parts

        def per_block(q_block):
            scores = jnp.dot(q_block, k_head.T, preferred_element_type=jnp.float32) * scale
            top = lax.optimization_barrier(jnp.max(scores, axis=-1, keepdims=True))
            lse = top + jnp.log(lax.optimization_barrier(jnp.sum(jnp.exp(scores - top), axis=-1, keepdims=True)))
            weights = jnp.exp(scores - lse)
            result = jnp.dot(weights, v_head.astype(jnp.float32))
            return (result.astype(jnp.bfloat16), lse[:, 0])
        result, lse = lax.map(per_block, q_head.reshape(count, block, DH))
        return (result.reshape(length, DH), lse.reshape(length))
    result, lse = lax.map(per_head, (split_heads(query), split_heads(keys), split_heads(values)))
    return (merge_heads(result), lse)

def attend_back(query, keys, values, attended, lse, d_att):
    length = query.shape[0]
    block = math.gcd(length, 512)
    count = length // block
    scale = DH ** (-0.5)
    delta = (d_att.astype(jnp.float32) * attended.astype(jnp.float32)).reshape(length, H, DH).sum(-1).T

    def per_head(parts):
        q_head, k_head, v_head, do_head, lse_head, delta_head = parts

        def per_block(carry, blocks):
            k_grad, v_grad = carry
            q_block, do_block, lse_block, delta_block = blocks
            scores = jnp.dot(q_block, k_head.T, preferred_element_type=jnp.float32) * scale
            weights = jnp.exp(scores - lse_block[:, None])
            weights_round = weights.astype(jnp.bfloat16)
            v_grad = v_grad + jnp.dot(weights_round.T, do_block, preferred_element_type=jnp.float32)
            d_weights = jnp.dot(do_block, v_head.T, preferred_element_type=jnp.float32)
            d_scores = (weights * (d_weights - delta_block[:, None])).astype(jnp.bfloat16)
            q_grad = (jnp.dot(d_scores, k_head, preferred_element_type=jnp.float32) * scale).astype(jnp.bfloat16)
            k_grad = k_grad + jnp.dot(d_scores.T, q_block, preferred_element_type=jnp.float32) * scale
            return ((k_grad, v_grad), q_grad)
        zeros = jnp.zeros((length, DH), jnp.float32)
        (k_grad, v_grad), q_grad = lax.scan(per_block, (zeros, zeros), (q_head.reshape(count, block, DH), do_head.reshape(count, block, DH), lse_head.reshape(count, block), delta_head.reshape(count, block)))
        return (q_grad.reshape(length, DH), k_grad.astype(jnp.bfloat16), v_grad.astype(jnp.bfloat16))
    q_grad, k_grad, v_grad = lax.map(per_head, (split_heads(query), split_heads(keys), split_heads(values), split_heads(d_att), lse, delta))
    return (merge_heads(q_grad), merge_heads(k_grad), merge_heads(v_grad))

def mat(left, right):
    return jnp.dot(left, right, preferred_element_type=jnp.float32)

def reference(tokens, query_weight, key_weight, value_weight, out_weight, query_bias, value_bias, out_bias, norm1_gain, norm1_shift, inner_weight, inner_bias, outer_weight, outer_bias, norm2_gain, norm2_shift, out_grad):
    gain_one = norm1_gain.astype(jnp.float32)
    gain_two = norm2_gain.astype(jnp.float32)
    bias_query = query_bias.reshape(-1).astype(jnp.float32)
    bias_value = value_bias.reshape(-1).astype(jnp.float32)
    bias_inner = inner_bias.reshape(-1).astype(jnp.float32)
    totals = None
    outputs = []
    in_grads = []
    for seq in range(SEQS):
        rows_in = tokens[seq]
        query = (mat(rows_in, query_weight) + bias_query).astype(jnp.bfloat16)
        keys = mat(rows_in, key_weight).astype(jnp.bfloat16)
        values = (mat(rows_in, value_weight) + bias_value).astype(jnp.bfloat16)
        attended, lse = attend(query, keys, values)
        resid_one = rows_in.astype(jnp.float32) + mat(attended, out_weight) + out_bias.astype(jnp.float32)
        normed_one, unit_one, rstd_one = norm_forward(resid_one, gain_one, norm1_shift.astype(jnp.float32))
        normed_round = normed_one.astype(jnp.bfloat16)
        pre_act = mat(normed_round, inner_weight) + bias_inner
        act_full, slope = gelu_parts(pre_act)
        activation = act_full.astype(jnp.bfloat16)
        resid_two = normed_one + mat(activation, outer_weight) + outer_bias.astype(jnp.float32)
        final, unit_two, rstd_two = norm_forward(resid_two, gain_two, norm2_shift.astype(jnp.float32))
        outputs.append(final.astype(jnp.bfloat16))
        d_resid_two, g_gain_two, g_shift_two = norm_backward(out_grad[seq].astype(jnp.float32), unit_two, rstd_two, gain_two)
        d_two_round = d_resid_two.astype(jnp.bfloat16)
        g_outer_w = mat(activation.T, d_two_round)
        g_outer_b = lax.optimization_barrier(jnp.sum(d_resid_two, axis=0))
        d_pre = mat(d_two_round, outer_weight.T) * slope
        d_pre_round = d_pre.astype(jnp.bfloat16)
        g_inner_w = mat(normed_round.T, d_pre_round)
        g_inner_b = lax.optimization_barrier(jnp.sum(d_pre, axis=0)).reshape(FF // DH, DH)
        d_normed = d_resid_two + mat(d_pre_round, inner_weight.T)
        d_resid_one, g_gain_one, g_shift_one = norm_backward(d_normed, unit_one, rstd_one, gain_one)
        d_one_round = d_resid_one.astype(jnp.bfloat16)
        g_out_w = mat(attended.T, d_one_round)
        g_out_b = lax.optimization_barrier(jnp.sum(d_resid_one, axis=0))
        d_att = mat(d_one_round, out_weight.T).astype(jnp.bfloat16)
        q_grad, k_grad, v_grad = attend_back(query, keys, values, attended, lse, d_att)
        g_query_w = mat(rows_in.T, q_grad)
        g_key_w = mat(rows_in.T, k_grad)
        g_value_w = mat(rows_in.T, v_grad)
        g_query_b = lax.optimization_barrier(jnp.sum(q_grad.astype(jnp.float32), axis=0)).reshape(H, DH)
        g_value_b = lax.optimization_barrier(jnp.sum(v_grad.astype(jnp.float32), axis=0)).reshape(H, DH)
        back = d_resid_one + mat(q_grad, query_weight.T) + mat(k_grad, key_weight.T) + mat(v_grad, value_weight.T)
        in_grads.append(back.astype(jnp.bfloat16))
        terms = (g_query_w, g_key_w, g_value_w, g_out_w, g_query_b, g_value_b, g_out_b, g_gain_one, g_shift_one, g_inner_w, g_inner_b, g_outer_w, g_outer_b, g_gain_two, g_shift_two)
        if totals is None:
            totals = terms
        else:
            totals = tuple((a + b for a, b in zip(totals, terms)))
    return (jnp.stack(outputs), jnp.stack(in_grads), totals[0], totals[1], totals[2], totals[3], totals[4], totals[5], totals[6], totals[7], totals[8], totals[9], totals[10], totals[11], totals[12], totals[13], totals[14])
```

```python
import math

import jax
import jax.numpy as jnp
from jax import lax
from jax.experimental import pallas as pl
from jax.experimental.pallas import tpu as pltpu
from jax.sharding import PartitionSpec as P

DH = 64


EPSILON = 1e-05


def gelu_parts(pre):
    cdf = 0.5 * (1.0 + lax.erf(pre * 0.7071067811865476))
    dens = jnp.exp(-0.5 * pre * pre) * 0.3989422804014327
    return (pre * cdf, cdf + pre * dens)


def norm_forward(resid, gain, shift):
    centre = resid - jnp.mean(resid, axis=-1, keepdims=True)
    rstd = lax.rsqrt(jnp.mean(centre * centre, axis=-1, keepdims=True) + EPSILON)
    unit = centre * rstd
    return (unit * gain + shift, unit, rstd)


def norm_backward(grad, unit, rstd, gain):
    scaled = grad * gain
    inner = (
        scaled
        - jnp.mean(scaled, axis=-1, keepdims=True)
        - unit * jnp.mean(scaled * unit, axis=-1, keepdims=True)
    )
    return (rstd * inner, jnp.sum(grad * unit, axis=0), jnp.sum(grad, axis=0))


def mat(left, right):
    return jnp.dot(left, right, preferred_element_type=jnp.float32)


MESH = pl.DeviceIdType.MESH
ORDER = ("dp", "blk", "ulysses")


def here():
    return {name: lax.axis_index(name) for name in ORDER}


def bits_of(axes):
    bits = []
    below = 1
    for name in reversed(axes):
        size = lax.axis_size(name)
        stride = 1
        while stride < size:
            bits.append((name, stride, stride * below))
            stride *= 2
        below *= size
    return bits


def slot_of(axes, at):
    index = 0
    for name in axes:
        index = index * lax.axis_size(name) + at[name]
    return index


def flip(index, stride):
    return index + stride * (1 - 2 * ((index // stride) % 2))


def flip_all(index, bits):
    for bit in bits:
        index = flip(index, bit[2])
    return index


def peer(at, bit):
    name, stride, unused = bit
    return tuple(flip(at[axis], stride) if axis == name else at[axis] for axis in ORDER)


def subsets(bits):
    found = [()]
    for bit in bits:
        found = found + [sub + (bit,) for sub in found]
    return found


def row_parts(rows, size, tile):
    if size < 65536 or rows % (2 * tile):
        return [(0, rows)]
    return [(0, rows // 2), (rows // 2, rows // 2)]


def row_loop(rows, body):
    step = math.gcd(rows, 64)

    def turn(i, carry):
        body(pl.ds(pl.multiple_of(i * step, step), step))
        return carry

    lax.fori_loop(0, rows // step, turn, 0)


class Sems:
    def __init__(self, ref=None):
        self.ref, self.count = ref, 0

    def take(self):
        self.count += 1
        return self.count - 1 if self.ref is None else self.ref.at[self.count - 1]


def remote(src, dst, sems, to):
    return pltpu.make_async_remote_copy(
        src_ref=src, dst_ref=dst, send_sem=sems[0], recv_sem=sems[1], device_id=to, device_id_type=MESH
    )


class CubeGather:
    def __init__(self, axes, arrays):
        self.axes, self.arrays, self.bits = axes, list(arrays), bits_of(axes)
        self.slots = math.prod(lax.axis_size(name) for name in axes)
        self.outs = [jax.ShapeDtypeStruct((self.slots,) + a.shape, a.dtype) for a in self.arrays]
        self.scratch = []
        streams = sum(len(self.parts(a)) for a in self.arrays)
        self.sems = 2 * streams * (self.slots - 1)

    def parts(self, array):
        return row_parts(array.shape[0], array.size, 16)

    def peers(self, at):
        return [(peer(at, bit), None) for bit in self.bits]

    def run(self, at, ins, outs, scratch, sems):
        gens = []
        me = slot_of(self.axes, at)
        for array, src, dst in zip(self.arrays, ins, outs):
            for number, part in enumerate(self.parts(array)):
                far = self.bits[1:]
                order = (far if number else far[::-1]) + self.bits[:1]
                gens.append(self.stream(at, me, src, dst, part, order, sems))
        yield from together(gens)
        for src, dst in zip(ins, outs):
            dst[me] = src[...]

    def stream(self, at, me, src, dst, part, order, sems):
        rows = pl.ds(*part)
        held, landing, sent = [()], {}, []
        for bit in order:
            fresh = {}
            for sub in held:
                if sub in landing:
                    landing.pop(sub).wait_recv()
                slot = flip_all(me, sub)
                there = dst.at[slot, rows]
                copy = remote(
                    there if sub else src.at[rows], there, (sems.take(), sems.take()), peer(at, bit)
                )
                copy.start()
                sent.append(copy)
                fresh[sub + (bit,)] = copy
            landing.update(fresh)
            held = held + list(fresh)
            yield
        for copy in landing.values():
            copy.wait_recv()
        for copy in sent:
            copy.wait_send()


class CubeScatter:
    def __init__(self, axes, arrays):
        self.axes, self.arrays, self.bits = axes, list(arrays), bits_of(axes)
        self.slots = math.prod(lax.axis_size(name) for name in axes)
        self.outs = [jax.ShapeDtypeStruct(a.shape[1:], jnp.float32) for a in self.arrays]
        self.scratch = []
        self.sems = 0
        for a in self.arrays:
            for part in self.parts(a):
                left = self.slots
                for unused in self.bits:
                    left //= 2
                    self.scratch.append(((left, part[1], a.shape[2]), a.dtype))
                    if left > 1:
                        self.scratch.append(((left, part[1], a.shape[2]), a.dtype))
                self.sems += 2 * (self.slots - 1)

    def parts(self, array):
        return row_parts(array.shape[1], array.size // self.slots, 16)

    def peers(self, at):
        return [(peer(at, bit), None) for bit in self.bits]

    def run(self, at, ins, outs, scratch, sems):
        gens = []
        me = slot_of(self.axes, at)
        scratch = list(scratch)
        for array, src, dst in zip(self.arrays, ins, outs):
            for number, part in enumerate(self.parts(array)):
                far = self.bits[1:]
                order = self.bits[:1] + (far if number else far[::-1])
                own = scratch[: 2 * len(order) - 1]
                scratch = scratch[2 * len(order) - 1 :]
                gens.append(self.stream(at, me, src, dst, part, order, own, sems))
        yield from together(gens)

    def stream(self, at, me, src, dst, part, order, scratch, sems):
        start, count = part
        rows = pl.ds(start, count)
        level = None
        sent = []
        for stage, bit in enumerate(order):
            rest = order[stage + 1 :]
            subs = subsets(rest)
            before = subsets(order[stage:])
            landed = scratch[2 * stage]
            copies = []
            for j, sub in enumerate(subs):
                if level is None:
                    piece = src.at[flip_all(flip(me, bit[2]), sub), rows]
                else:
                    piece = level.at[before.index((bit,) + sub)]
                copy = remote(piece, landed.at[j], (sems.take(), sems.take()), peer(at, bit))
                copy.start()
                copies.append(copy)
            sent += copies
            yield
            goal = None if not rest else scratch[2 * stage + 1]
            for j, sub in enumerate(subs):
                copies[j].wait_recv()
                slot = None if level is not None else flip_all(me, sub)
                old = None if level is None else before.index(sub)

                def add(here_rows, j=j, slot=slot, old=old, level=level, goal=goal, landed=landed):
                    moved = pl.ds(start + here_rows.start, here_rows.size)
                    mine = src[slot, moved, :] if level is None else level[old, here_rows, :]
                    total = mine.astype(jnp.float32) + landed[j, here_rows, :].astype(jnp.float32)
                    if goal is None:
                        dst[moved, :] = total
                    else:
                        goal[j, here_rows, :] = total.astype(goal.dtype)

                row_loop(count, add)
            level = goal
        for copy in sent:
            copy.wait_send()


def line_peers(at, size):
    spot = at["ulysses"]
    return [
        ((at["dp"], at["blk"], spot + 1), spot < size - 1),
        ((at["dp"], at["blk"], spot - 1), spot > 0),
    ]


class LineGather:
    def __init__(self, arrays):
        self.arrays, self.size = list(arrays), lax.axis_size("ulysses")
        self.outs = [jax.ShapeDtypeStruct((self.size,) + a.shape, a.dtype) for a in self.arrays]
        self.scratch = []
        streams = sum(len(self.parts(a)) for a in self.arrays)
        self.sems = streams * 4 * (self.size - 1)

    def parts(self, array):
        return row_parts(array.shape[0], array.size, 16)

    def peers(self, at):
        return line_peers(at, self.size)

    def run(self, at, ins, outs, scratch, sems):
        gens = [
            self.stream(at, src, dst, part, sems)
            for array, src, dst in zip(self.arrays, ins, outs)
            for part in self.parts(array)
        ]
        yield from together(gens)
        for src, dst in zip(ins, outs):
            dst[at["ulysses"]] = src[...]

    def stream(self, at, src, dst, part, sems):
        size, spot = self.size, at["ulysses"]
        rows = pl.ds(*part)
        ways = []
        for sign in (1, -1):
            tail = spot if sign > 0 else size - 1 - spot
            to = (at["dp"], at["blk"], spot + sign)
            pairs = [(sems.take(), sems.take()) for unused in range(size - 1)]
            ways.append((sign, tail, to, pairs))

        def copy(way, step):
            sign, tail, to, pairs = way
            slot = spot - sign * step
            there = dst.at[slot, rows]
            return remote(src.at[rows] if step == 0 else there, there, pairs[step], to)

        for step in range(size):
            for way in ways:
                tail = way[1]
                if step > 0:

                    @pl.when(tail >= step)
                    def unused_wait(way=way, step=step):
                        copy(way, step - 1).wait_recv()

                if step < size - 1:

                    @pl.when(jnp.logical_and(tail < size - 1, tail >= step))
                    def unused_send(way=way, step=step):
                        copy(way, step).start()

            yield
        for way in ways:
            for step in range(size - 1):

                @pl.when(jnp.logical_and(way[1] < size - 1, way[1] >= step))
                def unused_sent(way=way, step=step):
                    copy(way, step).wait_send()


class LineScatter:
    def __init__(self, arrays):
        self.arrays, self.size = list(arrays), lax.axis_size("ulysses")
        self.outs = [jax.ShapeDtypeStruct(a.shape[1:], jnp.float32) for a in self.arrays]
        self.scratch = []
        self.sems = 0
        for a in self.arrays:
            for part in self.parts(a):
                shape = (2, 2, self.size - 1, part[1], a.shape[2])
                self.scratch.append((shape, a.dtype))
                self.sems += 4 * (self.size - 1)

    def parts(self, array):
        return row_parts(array.shape[1], array.size // self.size, 16)

    def peers(self, at):
        return line_peers(at, self.size)

    def run(self, at, ins, outs, scratch, sems):
        gens, scratch = [], list(scratch)
        for array, src, dst in zip(self.arrays, ins, outs):
            for part in self.parts(array):
                gens.append(self.stream(at, src, dst, part, scratch.pop(0), sems))
        yield from together(gens)

    def stream(self, at, src, dst, part, room, sems):
        size, spot = self.size, at["ulysses"]
        start, count = part
        ways = []
        for index, sign in enumerate((1, -1)):
            tail = spot if sign > 0 else size - 1 - spot
            to = (at["dp"], at["blk"], spot + sign)
            pairs = [(sems.take(), sems.take()) for unused in range(size - 1)]
            ways.append((index, sign, tail, to, pairs))

        def owner(way, step):
            return spot + way[1] * (size - 1 - step)

        def copy(way, step, first):
            index, sign, tail, to, pairs = way
            piece = src.at[owner(way, step), pl.ds(start, count)] if first else room.at[index, 1, step]
            return remote(piece, room.at[index, 0, step], pairs[step], to)

        for step in range(size - 1):
            for way in ways:

                @pl.when(way[2] == 0)
                def unused_first(way=way, step=step):
                    copy(way, step, True).start()

                if step > 0:

                    @pl.when(jnp.logical_and(way[2] >= 1, way[2] <= step))
                    def unused_next(way=way, step=step):
                        index = way[0]
                        copy(way, step - 1, False).wait_recv()

                        def add(rows):
                            moved = pl.ds(start + rows.start, rows.size)
                            total = src[owner(way, step), moved, :].astype(jnp.float32) + room[
                                index, 0, step - 1, rows, :
                            ].astype(jnp.float32)
                            room[index, 1, step, rows, :] = total.astype(room.dtype)

                        row_loop(count, add)
                        copy(way, step, False).start()

            yield

        def begin(rows):
            moved = pl.ds(start + rows.start, rows.size)
            dst[moved, :] = src[spot, moved, :].astype(jnp.float32)

        row_loop(count, begin)
        for way in ways:

            @pl.when(way[2] >= 1)
            def unused_last(way=way):
                copy(way, size - 2, False).wait_recv()

                def add(rows):
                    moved = pl.ds(start + rows.start, rows.size)
                    dst[moved, :] = dst[moved, :] + room[way[0], 0, size - 2, rows, :].astype(jnp.float32)

                row_loop(count, add)

        for way in ways:
            for step in range(size - 1):

                @pl.when(way[2] == 0)
                def unused_sent_first(way=way, step=step):
                    copy(way, step, True).wait_send()

                if step > 0:

                    @pl.when(jnp.logical_and(way[2] >= 1, way[2] <= step))
                    def unused_sent(way=way, step=step):
                        copy(way, step, False).wait_send()


def together(gens):
    gens = list(gens)
    while gens:
        alive = []
        for gen in gens:
            try:
                next(gen)
                alive.append(gen)
            except StopIteration:
                pass
        gens = alive
        if gens:
            yield


def communicate(number, tasks):
    arrays = [a for task in tasks for a in task.arrays]
    outs = [o for task in tasks for o in task.outs]
    rooms = [s for task in tasks for s in task.scratch]
    count = sum(task.sems for task in tasks)

    def kernel(*refs):
        ins, refs = refs[: len(arrays)], refs[len(arrays) :]
        results, refs = refs[: len(outs)], refs[len(outs) :]
        scratch, sem_ref = refs[: len(rooms)], refs[len(rooms)]
        at = here()
        barrier = pltpu.get_barrier_semaphore()
        total = 0
        seen = set()
        for task in tasks:
            kind = type(task) in (LineGather, LineScatter)
            for place, (to, exists) in enumerate(task.peers(at)):
                name = ("line", place) if kind else task.bits[place][:2]
                if name in seen:
                    continue
                seen.add(name)
                if exists is None:
                    pl.semaphore_signal(barrier, inc=1, device_id=to, device_id_type=MESH)
                    total = total + 1
                else:

                    @pl.when(exists)
                    def unused_greet(to=to):
                        pl.semaphore_signal(barrier, inc=1, device_id=to, device_id_type=MESH)

                    total = total + exists.astype(jnp.int32)
        pl.semaphore_wait(barrier, total)
        sems = Sems(sem_ref)
        gens = []
        for task in tasks:
            n_in, n_out, n_room = len(task.arrays), len(task.outs), len(task.scratch)
            gens.append(task.run(at, ins[:n_in], results[:n_out], scratch[:n_room], sems))
            ins, results, scratch = ins[n_in:], results[n_out:], scratch[n_room:]
        for unused in together(gens):
            pass

    flat = pl.pallas_call(
        kernel,
        name="exchange_%d" % number,
        out_shape=outs,
        in_specs=[pl.BlockSpec(memory_space=pltpu.VMEM)] * len(arrays),
        out_specs=[pl.BlockSpec(memory_space=pltpu.VMEM)] * len(outs),
        scratch_shapes=[pltpu.VMEM(*room) for room in rooms] + [pltpu.SemaphoreType.DMA((count,))],
        compiler_params=pltpu.CompilerParams(collective_id=number, has_side_effects=True),
    )(*arrays)
    flat = list(flat)
    split = []
    for task in tasks:
        split.append(flat[: len(task.outs)])
        flat = flat[len(task.outs) :]
    return split


def pack(pieces, slots):
    joined = jnp.concatenate([p.astype(jnp.float32) for p in pieces], axis=1)
    length = joined.shape[1]
    padded = -(-length // 1024) * 1024
    return jnp.pad(joined, ((0, 0), (0, padded - length))).reshape(slots, padded // 128, 128)


def row_slots(grad, slots):
    return grad.astype(jnp.bfloat16).reshape(slots, -1, grad.shape[1])


def column_slots(grad, slots):
    return grad.astype(jnp.bfloat16).reshape(grad.shape[0], slots, -1).transpose(1, 0, 2)


def spread_rows(vectors, lanes):
    rows = jnp.pad(jnp.stack(vectors), ((0, -len(vectors) % 8), (0, 0)))
    return jnp.broadcast_to(rows[None], (lanes,) + rows.shape)


def attend_forward(q_heads, k_all, v_all, heads_dev):
    rows, head_width = q_heads.shape
    scale = DH ** (-0.5)
    q_three = q_heads.reshape(rows, heads_dev, DH)

    def fold(carry, piece, start):
        k_piece, v_piece = piece
        count = k_piece.shape[0]
        size = math.gcd(count, 512)
        steps = count // size
        k_split = k_piece.reshape(steps, size, heads_dev, DH)
        v_split = v_piece.reshape(steps, size, heads_dev, DH)

        def step(state, blocks):
            best, total, accum = state
            k_block, v_block = blocks
            scores = (
                jnp.einsum("qhd,khd->hqk", q_three, k_block, preferred_element_type=jnp.float32)
                * scale
            )
            new_best = jnp.maximum(best, jnp.max(scores, axis=-1))
            fade = jnp.exp(best - new_best)
            weights = jnp.exp(scores - new_best[:, :, None])
            total = total * fade + jnp.sum(weights, axis=-1)
            update = jnp.einsum("hqk,khd->qhd", weights, v_block.astype(jnp.float32))
            accum = accum.reshape(rows, heads_dev, DH) * fade.T[:, :, None] + update
            return ((new_best, total, accum.reshape(rows, head_width)), None)

        state, unused = lax.scan(step, carry, (k_split, v_split))
        return state

    start_state = (
        jnp.full((heads_dev, rows), -jnp.inf, jnp.float32),
        jnp.zeros((heads_dev, rows), jnp.float32),
        jnp.zeros((rows, head_width), jnp.float32),
    )
    best, total, accum = fold(
        start_state,
        (
            k_all,
            v_all,
        ),
        jnp.int32(0),
    )
    attended = (accum.reshape(rows, heads_dev, DH) / total.T[:, :, None]).reshape(rows, head_width)
    return (attended.astype(jnp.bfloat16), best + jnp.log(total))


def attend_backward(q_heads, k_all, v_all, attended, lse, d_att, heads_dev):
    rows, head_width = q_heads.shape
    scale = DH ** (-0.5)
    q_three = q_heads.reshape(rows, heads_dev, DH)
    do_three = d_att.reshape(rows, heads_dev, DH)
    delta = (
        (d_att.astype(jnp.float32) * attended.astype(jnp.float32))
        .reshape(rows, heads_dev, DH)
        .sum(-1)
        .T
    )
    all_keys = rows * lax.axis_size("blk")

    def fold(carry, piece, start):
        dq_accum, key_accum = carry
        k_piece, v_piece = piece
        count = k_piece.shape[0]
        size = math.gcd(count, 512)
        steps = count // size
        k_split = k_piece.reshape(steps, size, heads_dev, DH)
        v_split = v_piece.reshape(steps, size, heads_dev, DH)

        def step(dq_state, blocks):
            k_block, v_block = blocks
            scores = (
                jnp.einsum("qhd,khd->hqk", q_three, k_block, preferred_element_type=jnp.float32)
                * scale
            )
            weights = jnp.exp(scores - lse[:, :, None])
            weights_round = weights.astype(jnp.bfloat16)
            v_part = jnp.einsum(
                "hqk,qhd->khd", weights_round, do_three, preferred_element_type=jnp.float32
            )
            d_weights = jnp.einsum(
                "qhd,khd->hqk", do_three, v_block, preferred_element_type=jnp.float32
            )
            d_scores = (weights * (d_weights - delta[:, :, None])).astype(jnp.bfloat16)
            q_part = (
                jnp.einsum("hqk,khd->qhd", d_scores, k_block, preferred_element_type=jnp.float32)
                * scale
            )
            k_part = (
                jnp.einsum("hqk,qhd->khd", d_scores, q_three, preferred_element_type=jnp.float32)
                * scale
            )
            dq_state = dq_state + q_part.reshape(rows, head_width)
            both = (
                k_part.reshape(size, head_width).astype(jnp.bfloat16),
                v_part.reshape(size, head_width).astype(jnp.bfloat16),
            )
            return (dq_state, both)

        dq_accum, parts = lax.scan(step, dq_accum, (k_split, v_split))
        return (dq_accum, parts)

    start_state = (
        jnp.zeros((rows, head_width), jnp.float32),
        None,
    )
    dq_accum, key_accum = fold(
        start_state,
        (
            k_all,
            v_all,
        ),
        jnp.int32(0),
    )
    blocks = lax.axis_size("blk")
    owned = communicate(
        8, [CubeScatter(("blk",), [part.reshape(blocks, rows, head_width) for part in key_accum])]
    )[0]
    return (
        dq_accum.astype(jnp.bfloat16),
        owned[0].astype(jnp.bfloat16),
        owned[1].astype(jnp.bfloat16),
    )


def local(
    tokens,
    query_weight,
    key_weight,
    value_weight,
    out_weight,
    query_bias,
    value_bias,
    out_bias,
    norm1_gain,
    norm1_shift,
    inner_weight,
    inner_bias,
    outer_weight,
    outer_bias,
    norm2_gain,
    norm2_shift,
    out_grad,
):
    group = ("dp", "blk")
    slots = lax.axis_size("dp") * lax.axis_size("blk")
    blocks = lax.axis_size("blk")
    lanes = lax.axis_size("ulysses")
    rows_in = tokens[0]
    tok_rows, width = rows_in.shape
    head_width = query_weight.shape[1]
    heads_dev = head_width // DH
    inner_width = inner_weight.shape[1]
    small_in = (
        out_bias,
        norm1_gain,
        norm1_shift,
        outer_bias,
        norm2_gain,
        norm2_shift,
        query_bias,
        value_bias,
        inner_bias,
    )
    (tok_all,), (q3, k3, v3, o3, small) = communicate(
        0,
        [
            LineGather([rows_in]),
            CubeGather(
                group,
                [
                    query_weight,
                    key_weight,
                    value_weight,
                    out_weight,
                    pack([a.reshape(1, -1) for a in small_in], 1)[0],
                ],
            ),
        ],
    )
    rows_all = tok_all.reshape(-1, width)
    w_query, w_key, w_value = (w.reshape(width, head_width) for w in (q3, k3, v3))
    w_out = o3.transpose(1, 0, 2).reshape(head_width, width)
    flat = small.reshape(slots, -1)
    vectors = []
    start = 0
    for a in small_in:
        piece = flat[:, start : start + a.size]
        start += a.size
        if a.ndim == 2:
            piece = piece.reshape((slots,) + a.shape).transpose(1, 0, 2)
        vectors.append(piece.reshape(-1))
    b_out, gain_one, shift_one, b_outer, gain_two, shift_two, b_query, b_value, b_inner = vectors
    q_heads = (mat(rows_all, w_query) + b_query).astype(jnp.bfloat16)
    k_heads = mat(rows_all, w_key).astype(jnp.bfloat16)
    v_heads = (mat(rows_all, w_value) + b_value).astype(jnp.bfloat16)
    k_all, v_all = communicate(1, [CubeGather(("blk",), [k_heads, v_heads])])[0]
    k_all = k_all.reshape(-1, head_width)
    v_all = v_all.reshape(-1, head_width)
    attended, lse = attend_forward(q_heads, k_all, v_all, heads_dev)
    (attn_sum,), (inner3, outer3) = communicate(
        2,
        [
            LineScatter([mat(attended, w_out).astype(jnp.bfloat16).reshape(lanes, tok_rows, width)]),
            CubeGather(group, [inner_weight, outer_weight]),
        ],
    )
    w_inner = inner3.reshape(width, inner_width)
    w_outer = outer3.transpose(1, 0, 2).reshape(inner_width, width)
    resid_one = rows_in.astype(jnp.float32) + attn_sum + b_out
    normed_one, unit_one, rstd_one = norm_forward(
        resid_one, gain_one, shift_one
    )
    normed_round = normed_one.astype(jnp.bfloat16)
    normed_all = communicate(3, [LineGather([normed_round])])[0][0].reshape(-1, width)
    pre_act = mat(normed_all, w_inner) + b_inner
    act_full, slope = gelu_parts(pre_act)
    activation = act_full.astype(jnp.bfloat16)
    ffn_term = mat(activation, w_outer).astype(jnp.bfloat16).reshape(lanes, tok_rows, width)
    ffn_sum = communicate(4, [LineScatter([ffn_term])])[0][0]
    resid_two = normed_one + ffn_sum + b_outer
    final, unit_two, rstd_two = norm_forward(
        resid_two, gain_two, shift_two
    )
    block_out = final.astype(jnp.bfloat16)[None]
    d_resid_two, g_gain_two, g_shift_two = norm_backward(
        out_grad[0].astype(jnp.float32), unit_two, rstd_two, gain_two
    )
    g_outer_b = jnp.sum(d_resid_two, axis=0)
    d_two_round = d_resid_two.astype(jnp.bfloat16)
    d_two_all = communicate(5, [LineGather([d_two_round])])[0][0].reshape(-1, width)
    g_outer_w = jnp.einsum("tf,td->fd", activation, d_two_all, preferred_element_type=jnp.float32)
    d_pre = jnp.einsum("td,fd->tf", d_two_all, w_outer, preferred_element_type=jnp.float32) * slope
    d_pre_round = d_pre.astype(jnp.bfloat16)
    g_inner_w = jnp.einsum("td,tf->df", normed_all, d_pre_round, preferred_element_type=jnp.float32)
    g_inner_b = jnp.sum(d_pre, axis=0).reshape(-1, DH)
    extras_two = spread_rows([g_gain_two, g_shift_two, g_outer_b], lanes)
    d_term = jnp.einsum("tf,df->td", d_pre_round, w_inner, preferred_element_type=jnp.float32)
    (d_sum, sums_two), (r_outer,) = communicate(
        6,
        [
            LineScatter([d_term.astype(jnp.bfloat16).reshape(lanes, tok_rows, width), extras_two]),
            CubeScatter(group, [column_slots(g_outer_w, slots)]),
        ],
    )
    d_normed = d_resid_two + d_sum
    d_resid_one, g_gain_one, g_shift_one = norm_backward(
        d_normed, unit_one, rstd_one, gain_one
    )
    g_out_b = jnp.sum(d_resid_one, axis=0)
    d_one_round = d_resid_one.astype(jnp.bfloat16)
    (d_one_all,), (r_inner,) = communicate(
        7,
        [LineGather([d_one_round]), CubeScatter(group, [row_slots(g_inner_w, slots)])],
    )
    d_one_all = d_one_all.reshape(-1, width)
    g_out_w = jnp.einsum("te,td->ed", attended, d_one_all, preferred_element_type=jnp.float32)
    d_att = jnp.einsum("td,ed->te", d_one_all, w_out, preferred_element_type=jnp.float32).astype(
        jnp.bfloat16
    )
    dq_heads, dk_heads, dv_heads = attend_backward(
        q_heads, k_all, v_all, attended, lse, d_att, heads_dev
    )
    g_query_w = jnp.einsum("td,te->de", rows_all, dq_heads, preferred_element_type=jnp.float32)
    g_key_w = jnp.einsum("td,te->de", rows_all, dk_heads, preferred_element_type=jnp.float32)
    g_value_w = jnp.einsum("td,te->de", rows_all, dv_heads, preferred_element_type=jnp.float32)
    g_query_b = jnp.sum(dq_heads.astype(jnp.float32), axis=0).reshape(-1, DH)
    g_value_b = jnp.sum(dv_heads.astype(jnp.float32), axis=0).reshape(-1, DH)
    extras_one = spread_rows([g_gain_one, g_shift_one, g_out_b], lanes)
    back = None
    for grad, weight in ((dq_heads, w_query), (dk_heads, w_key), (dv_heads, w_value)):
        term = jnp.einsum("te,de->td", grad, weight, preferred_element_type=jnp.float32)
        back = term if back is None else back + term
    (back_sum, sums_one), (r_query, r_key, r_value, r_out) = communicate(
        9,
        [
            LineScatter([back.astype(jnp.bfloat16).reshape(lanes, tok_rows, width), extras_one]),
            CubeScatter(
                group,
                [
                    row_slots(g_query_w, slots),
                    row_slots(g_key_w, slots),
                    row_slots(g_value_w, slots),
                    column_slots(g_out_w, slots),
                ],
            ),
        ],
    )
    tokens_grad = (d_resid_one + back_sum).astype(jnp.bfloat16)[None]
    small_out = [v.reshape(slots, -1) for v in (*sums_one[:3], *sums_two[:3])]
    for bias in (g_query_b, g_value_b, g_inner_b):
        count = bias.shape[0]
        small_out.append(bias.reshape(count, slots, -1).transpose(1, 0, 2).reshape(slots, -1))
    kept = communicate(10, [CubeScatter(group, [pack(small_out, slots)])])[0][0].reshape(-1)
    ends = []
    start = 0
    for piece in small_out:
        ends.append(kept[start : start + piece.shape[1]])
        start += piece.shape[1]
    gain1, shift1, outb, gain2, shift2, outerb, queryb, valueb, innerb = ends
    return (
        block_out,
        tokens_grad,
        r_query,
        r_key,
        r_value,
        r_out,
        queryb.reshape(query_bias.shape),
        valueb.reshape(value_bias.shape),
        outb,
        gain1,
        shift1,
        r_inner,
        innerb.reshape(inner_bias.shape),
        r_outer,
        outerb,
        gain2,
        shift2,
    )


def solution(mesh):
    in_specs = (
        P("dp", ("blk", "ulysses"), None),
        P(("dp", "blk"), "ulysses"),
        P(("dp", "blk"), "ulysses"),
        P(("dp", "blk"), "ulysses"),
        P("ulysses", ("dp", "blk")),
        P("ulysses", ("dp", "blk")),
        P("ulysses", ("dp", "blk")),
        P(("dp", "blk")),
        P(("dp", "blk")),
        P(("dp", "blk")),
        P(("dp", "blk"), "ulysses"),
        P("ulysses", ("dp", "blk")),
        P("ulysses", ("dp", "blk")),
        P(("dp", "blk")),
        P(("dp", "blk")),
        P(("dp", "blk")),
        P("dp", ("blk", "ulysses"), None),
    )
    out_specs = (
        P("dp", ("blk", "ulysses"), None),
        P("dp", ("blk", "ulysses"), None),
        P(("dp", "blk"), "ulysses"),
        P(("dp", "blk"), "ulysses"),
        P(("dp", "blk"), "ulysses"),
        P("ulysses", ("dp", "blk")),
        P("ulysses", ("dp", "blk")),
        P("ulysses", ("dp", "blk")),
        P(("dp", "blk")),
        P(("dp", "blk")),
        P(("dp", "blk")),
        P(("dp", "blk"), "ulysses"),
        P("ulysses", ("dp", "blk")),
        P("ulysses", ("dp", "blk")),
        P(("dp", "blk")),
        P(("dp", "blk")),
        P(("dp", "blk")),
    )
    return jax.shard_map(local, mesh=mesh, in_specs=in_specs, out_specs=out_specs, check_vma=False)
```

```python
import math

import jax
import jax.numpy as jnp
from jax import lax
from jax.experimental import pallas as pl
from jax.experimental.pallas import tpu as pltpu
from jax.sharding import PartitionSpec as P

DH = 64


EPSILON = 1e-05


def gelu_parts(pre):
    cdf = 0.5 * (1.0 + lax.erf(pre * 0.7071067811865476))
    dens = jnp.exp(-0.5 * pre * pre) * 0.3989422804014327
    return (pre * cdf, cdf + pre * dens)


def norm_forward(resid, gain, shift):
    centre = resid - jnp.mean(resid, axis=-1, keepdims=True)
    rstd = lax.rsqrt(jnp.mean(centre * centre, axis=-1, keepdims=True) + EPSILON)
    unit = centre * rstd
    return (unit * gain + shift, unit, rstd)


def norm_backward(grad, unit, rstd, gain):
    scaled = grad * gain
    inner = (
        scaled
        - jnp.mean(scaled, axis=-1, keepdims=True)
        - unit * jnp.mean(scaled * unit, axis=-1, keepdims=True)
    )
    return (rstd * inner, jnp.sum(grad * unit, axis=0), jnp.sum(grad, axis=0))


def mat(left, right):
    return jnp.dot(left, right, preferred_element_type=jnp.float32)


MESH = pl.DeviceIdType.MESH
ORDER = ("dp", "blk", "ulysses")


def here():
    return {name: lax.axis_index(name) for name in ORDER}


def bits_of(axes):
    bits = []
    below = 1
    for name in reversed(axes):
        size = lax.axis_size(name)
        stride = 1
        while stride < size:
            bits.append((name, stride, stride * below))
            stride *= 2
        below *= size
    return bits


def slot_of(axes, at):
    index = 0
    for name in axes:
        index = index * lax.axis_size(name) + at[name]
    return index


def flip(index, stride):
    return index + stride * (1 - 2 * ((index // stride) % 2))


def flip_all(index, bits):
    for bit in bits:
        index = flip(index, bit[2])
    return index


def peer(at, bit):
    name, stride, unused = bit
    return tuple(flip(at[axis], stride) if axis == name else at[axis] for axis in ORDER)


def subsets(bits):
    found = [()]
    for bit in bits:
        found = found + [sub + (bit,) for sub in found]
    return found


def row_parts(rows, size, tile):
    if size < 65536 or rows % (2 * tile):
        return [(0, rows)]
    return [(0, rows // 2), (rows // 2, rows // 2)]


def row_loop(rows, body):
    step = math.gcd(rows, 64)

    def turn(i, carry):
        body(pl.ds(pl.multiple_of(i * step, step), step))
        return carry

    lax.fori_loop(0, rows // step, turn, 0)


class Sems:
    def __init__(self, ref=None):
        self.ref, self.count = ref, 0

    def take(self):
        self.count += 1
        return self.count - 1 if self.ref is None else self.ref.at[self.count - 1]


def remote(src, dst, sems, to):
    return pltpu.make_async_remote_copy(
        src_ref=src, dst_ref=dst, send_sem=sems[0], recv_sem=sems[1], device_id=to, device_id_type=MESH
    )


def slab(slot, width):
    return pl.ds(pl.multiple_of(slot * width, width), width)


def slot_rows(ref, slot, rows, width):
    return ref.at[slot, rows] if len(ref.shape) == 3 else ref.at[rows, slab(slot, width)]


class CubeGather:
    def __init__(self, axes, arrays, columns=(False,) * 8):
        self.axes, self.arrays, self.bits = axes, list(arrays), bits_of(axes)
        self.slots = math.prod(lax.axis_size(name) for name in axes)
        self.flat = [joined and a.shape[1] % 128 == 0 for a, joined in zip(self.arrays, columns)]
        self.outs = [
            jax.ShapeDtypeStruct(
                (a.shape[0], self.slots * a.shape[1]) if flat else (self.slots,) + a.shape, a.dtype
            )
            for a, flat in zip(self.arrays, self.flat)
        ]
        self.scratch = []
        streams = sum(len(self.parts(a)) for a in self.arrays)
        self.sems = 2 * streams * (self.slots - 1)

    def parts(self, array):
        return row_parts(array.shape[0], array.size, 16)

    def peers(self, at):
        return [(peer(at, bit), None) for bit in self.bits]

    def run(self, at, ins, outs, scratch, sems):
        gens = []
        me = slot_of(self.axes, at)
        for array, src, dst in zip(self.arrays, ins, outs):
            for number, part in enumerate(self.parts(array)):
                far = self.bits[1:]
                order = (far if number else far[::-1]) + self.bits[:1]
                gens.append(self.stream(at, me, src, dst, part, order, sems))
        yield from together(gens)
        for src, dst in zip(ins, outs):
            if len(dst.shape) == 2:
                dst[:, slab(me, src.shape[1])] = src[...]
            else:
                dst[me] = src[...]

    def stream(self, at, me, src, dst, part, order, sems):
        rows = pl.ds(*part)
        held, landing, sent = [()], {}, []
        for bit in order:
            fresh = {}
            for sub in held:
                if sub in landing:
                    landing.pop(sub).wait_recv()
                slot = flip_all(me, sub)
                there = slot_rows(dst, slot, rows, src.shape[1])
                copy = remote(
                    there if sub else src.at[rows], there, (sems.take(), sems.take()), peer(at, bit)
                )
                copy.start()
                sent.append(copy)
                fresh[sub + (bit,)] = copy
            landing.update(fresh)
            held = held + list(fresh)
            yield
        for copy in landing.values():
            copy.wait_recv()
        for copy in sent:
            copy.wait_send()


class CubeScatter:
    def __init__(self, axes, arrays):
        self.axes, self.arrays, self.bits = axes, list(arrays), bits_of(axes)
        self.slots = math.prod(lax.axis_size(name) for name in axes)
        self.outs = [jax.ShapeDtypeStruct(self.piece(a), jnp.float32) for a in self.arrays]
        self.scratch = []
        self.sems = 0
        for a in self.arrays:
            width = self.piece(a)[1]
            for part in self.parts(a):
                left = self.slots
                for unused in self.bits:
                    left //= 2
                    self.scratch.append(((left, part[1], width), a.dtype))
                    if left > 1:
                        self.scratch.append(((left, part[1], width), a.dtype))
                self.sems += 2 * (self.slots - 1)

    def piece(self, array):
        return array.shape[1:] if array.ndim == 3 else (array.shape[0], array.shape[1] // self.slots)

    def parts(self, array):
        return row_parts(self.piece(array)[0], array.size // self.slots, 16)

    def peers(self, at):
        return [(peer(at, bit), None) for bit in self.bits]

    def run(self, at, ins, outs, scratch, sems):
        gens = []
        me = slot_of(self.axes, at)
        scratch = list(scratch)
        for array, src, dst in zip(self.arrays, ins, outs):
            for number, part in enumerate(self.parts(array)):
                far = self.bits[1:]
                order = self.bits[:1] + (far if number else far[::-1])
                own = scratch[: 2 * len(order) - 1]
                scratch = scratch[2 * len(order) - 1 :]
                gens.append(self.stream(at, me, src, dst, part, order, own, sems))
        yield from together(gens)

    def stream(self, at, me, src, dst, part, order, scratch, sems):
        start, count = part
        rows = pl.ds(start, count)
        level = None
        sent = []
        for stage, bit in enumerate(order):
            rest = order[stage + 1 :]
            subs = subsets(rest)
            before = subsets(order[stage:])
            landed = scratch[2 * stage]
            copies = []
            for j, sub in enumerate(subs):
                if level is None:
                    piece = slot_rows(src, flip_all(flip(me, bit[2]), sub), rows, dst.shape[1])
                else:
                    piece = level.at[before.index((bit,) + sub)]
                copy = remote(piece, landed.at[j], (sems.take(), sems.take()), peer(at, bit))
                copy.start()
                copies.append(copy)
            sent += copies
            yield
            goal = None if not rest else scratch[2 * stage + 1]
            for j, sub in enumerate(subs):
                copies[j].wait_recv()
                slot = None if level is not None else flip_all(me, sub)
                old = None if level is None else before.index(sub)

                def add(here_rows, j=j, slot=slot, old=old, level=level, goal=goal, landed=landed):
                    moved = pl.ds(start + here_rows.start, here_rows.size)
                    if level is not None:
                        mine = level[old, here_rows, :]
                    elif len(src.shape) == 3:
                        mine = src[slot, moved, :]
                    else:
                        mine = src[moved, slab(slot, dst.shape[1])]
                    total = mine.astype(jnp.float32) + landed[j, here_rows, :].astype(jnp.float32)
                    if goal is None:
                        dst[moved, :] = total
                    else:
                        goal[j, here_rows, :] = total.astype(goal.dtype)

                row_loop(count, add)
            level = goal
        for copy in sent:
            copy.wait_send()


def line_peers(at, size):
    spot = at["ulysses"]
    return [
        ((at["dp"], at["blk"], spot + 1), spot < size - 1),
        ((at["dp"], at["blk"], spot - 1), spot > 0),
    ]


class LineGather:
    def __init__(self, arrays):
        self.arrays, self.size = list(arrays), lax.axis_size("ulysses")
        self.outs = [jax.ShapeDtypeStruct((self.size,) + a.shape, a.dtype) for a in self.arrays]
        self.scratch = []
        streams = sum(len(self.parts(a)) for a in self.arrays)
        self.sems = streams * 4 * (self.size - 1)

    def parts(self, array):
        return row_parts(array.shape[0], array.size, 16)

    def peers(self, at):
        return line_peers(at, self.size)

    def run(self, at, ins, outs, scratch, sems):
        gens = [
            self.stream(at, src, dst, part, sems)
            for array, src, dst in zip(self.arrays, ins, outs)
            for part in self.parts(array)
        ]
        yield from together(gens)
        for src, dst in zip(ins, outs):
            dst[at["ulysses"]] = src[...]

    def stream(self, at, src, dst, part, sems):
        size, spot = self.size, at["ulysses"]
        rows = pl.ds(*part)
        ways = []
        for sign in (1, -1):
            tail = spot if sign > 0 else size - 1 - spot
            to = (at["dp"], at["blk"], spot + sign)
            pairs = [(sems.take(), sems.take()) for unused in range(size - 1)]
            ways.append((sign, tail, to, pairs))

        def copy(way, step):
            sign, tail, to, pairs = way
            slot = spot - sign * step
            there = dst.at[slot, rows]
            return remote(src.at[rows] if step == 0 else there, there, pairs[step], to)

        for step in range(size):
            for way in ways:
                tail = way[1]
                if step > 0:

                    @pl.when(tail >= step)
                    def unused_wait(way=way, step=step):
                        copy(way, step - 1).wait_recv()

                if step < size - 1:

                    @pl.when(jnp.logical_and(tail < size - 1, tail >= step))
                    def unused_send(way=way, step=step):
                        copy(way, step).start()

            yield
        for way in ways:
            for step in range(size - 1):

                @pl.when(jnp.logical_and(way[1] < size - 1, way[1] >= step))
                def unused_sent(way=way, step=step):
                    copy(way, step).wait_send()


class LineScatter:
    def __init__(self, arrays):
        self.arrays, self.size = list(arrays), lax.axis_size("ulysses")
        self.outs = [jax.ShapeDtypeStruct(a.shape[1:], jnp.float32) for a in self.arrays]
        self.scratch = []
        self.sems = 0
        for a in self.arrays:
            for part in self.parts(a):
                shape = (2, 2, self.size - 1, part[1], a.shape[2])
                self.scratch.append((shape, a.dtype))
                self.sems += 4 * (self.size - 1)

    def parts(self, array):
        return row_parts(array.shape[1], array.size // self.size, 16)

    def peers(self, at):
        return line_peers(at, self.size)

    def run(self, at, ins, outs, scratch, sems):
        gens, scratch = [], list(scratch)
        for array, src, dst in zip(self.arrays, ins, outs):
            for part in self.parts(array):
                gens.append(self.stream(at, src, dst, part, scratch.pop(0), sems))
        yield from together(gens)

    def stream(self, at, src, dst, part, room, sems):
        size, spot = self.size, at["ulysses"]
        start, count = part
        ways = []
        for index, sign in enumerate((1, -1)):
            tail = spot if sign > 0 else size - 1 - spot
            to = (at["dp"], at["blk"], spot + sign)
            pairs = [(sems.take(), sems.take()) for unused in range(size - 1)]
            ways.append((index, sign, tail, to, pairs))

        def owner(way, step):
            return spot + way[1] * (size - 1 - step)

        def copy(way, step, first):
            index, sign, tail, to, pairs = way
            piece = src.at[owner(way, step), pl.ds(start, count)] if first else room.at[index, 1, step]
            return remote(piece, room.at[index, 0, step], pairs[step], to)

        for step in range(size - 1):
            for way in ways:

                @pl.when(way[2] == 0)
                def unused_first(way=way, step=step):
                    copy(way, step, True).start()

                if step > 0:

                    @pl.when(jnp.logical_and(way[2] >= 1, way[2] <= step))
                    def unused_next(way=way, step=step):
                        index = way[0]
                        copy(way, step - 1, False).wait_recv()

                        def add(rows):
                            moved = pl.ds(start + rows.start, rows.size)
                            total = src[owner(way, step), moved, :].astype(jnp.float32) + room[
                                index, 0, step - 1, rows, :
                            ].astype(jnp.float32)
                            room[index, 1, step, rows, :] = total.astype(room.dtype)

                        row_loop(count, add)
                        copy(way, step, False).start()

            yield

        def begin(rows):
            moved = pl.ds(start + rows.start, rows.size)
            dst[moved, :] = src[spot, moved, :].astype(jnp.float32)

        row_loop(count, begin)
        for way in ways:

            @pl.when(way[2] >= 1)
            def unused_last(way=way):
                copy(way, size - 2, False).wait_recv()

                def add(rows):
                    moved = pl.ds(start + rows.start, rows.size)
                    dst[moved, :] = dst[moved, :] + room[way[0], 0, size - 2, rows, :].astype(jnp.float32)

                row_loop(count, add)

        for way in ways:
            for step in range(size - 1):

                @pl.when(way[2] == 0)
                def unused_sent_first(way=way, step=step):
                    copy(way, step, True).wait_send()

                if step > 0:

                    @pl.when(jnp.logical_and(way[2] >= 1, way[2] <= step))
                    def unused_sent(way=way, step=step):
                        copy(way, step, False).wait_send()


def together(gens):
    gens = list(gens)
    while gens:
        alive = []
        for gen in gens:
            try:
                next(gen)
                alive.append(gen)
            except StopIteration:
                pass
        gens = alive
        if gens:
            yield


def communicate(number, tasks):
    arrays = [a for task in tasks for a in task.arrays]
    outs = [o for task in tasks for o in task.outs]
    rooms = [s for task in tasks for s in task.scratch]
    count = sum(task.sems for task in tasks)

    def kernel(*refs):
        ins, refs = refs[: len(arrays)], refs[len(arrays) :]
        results, refs = refs[: len(outs)], refs[len(outs) :]
        scratch, sem_ref = refs[: len(rooms)], refs[len(rooms)]
        at = here()
        barrier = pltpu.get_barrier_semaphore()
        total = 0
        seen = set()
        for task in tasks:
            kind = type(task) in (LineGather, LineScatter)
            for place, (to, exists) in enumerate(task.peers(at)):
                name = ("line", place) if kind else task.bits[place][:2]
                if name in seen:
                    continue
                seen.add(name)
                if exists is None:
                    pl.semaphore_signal(barrier, inc=1, device_id=to, device_id_type=MESH)
                    total = total + 1
                else:

                    @pl.when(exists)
                    def unused_greet(to=to):
                        pl.semaphore_signal(barrier, inc=1, device_id=to, device_id_type=MESH)

                    total = total + exists.astype(jnp.int32)
        pl.semaphore_wait(barrier, total)
        sems = Sems(sem_ref)
        gens = []
        for task in tasks:
            n_in, n_out, n_room = len(task.arrays), len(task.outs), len(task.scratch)
            gens.append(task.run(at, ins[:n_in], results[:n_out], scratch[:n_room], sems))
            ins, results, scratch = ins[n_in:], results[n_out:], scratch[n_room:]
        for unused in together(gens):
            pass

    flat = pl.pallas_call(
        kernel,
        name="exchange_%d" % number,
        out_shape=outs,
        in_specs=[pl.BlockSpec(memory_space=pltpu.VMEM)] * len(arrays),
        out_specs=[pl.BlockSpec(memory_space=pltpu.VMEM)] * len(outs),
        scratch_shapes=[pltpu.VMEM(*room) for room in rooms] + [pltpu.SemaphoreType.DMA((count,))],
        compiler_params=pltpu.CompilerParams(collective_id=number, has_side_effects=True),
    )(*arrays)
    flat = list(flat)
    split = []
    for task in tasks:
        split.append(flat[: len(task.outs)])
        flat = flat[len(task.outs) :]
    return split


def pack(pieces, slots):
    joined = jnp.concatenate([p.astype(jnp.float32) for p in pieces], axis=1)
    length = joined.shape[1]
    padded = -(-length // 1024) * 1024
    return jnp.pad(joined, ((0, 0), (0, padded - length))).reshape(slots, padded // 128, 128)


def row_slots(grad, slots):
    return grad.astype(jnp.bfloat16).reshape(slots, -1, grad.shape[1])


def column_slots(grad, slots):
    if grad.shape[1] % (128 * slots) == 0:
        return grad.astype(jnp.bfloat16)
    return grad.astype(jnp.bfloat16).reshape(grad.shape[0], slots, -1).transpose(1, 0, 2)


def join_columns(gathered):
    if gathered.ndim == 2:
        return gathered
    return gathered.transpose(1, 0, 2).reshape(gathered.shape[1], -1)


def spread_rows(vectors, lanes):
    rows = jnp.pad(jnp.stack(vectors), ((0, -len(vectors) % 8), (0, 0)))
    return jnp.broadcast_to(rows[None], (lanes,) + rows.shape)


def contract(left, right, sides):
    return lax.dot_general(left, right, ((sides[:1], sides[1:]), ((), ())), preferred_element_type=jnp.float32)


def heads_at_once(heads_dev):
    return 2 if heads_dev % 2 == 0 else heads_dev


def attend_forward(q_heads, k_all, v_all, heads_dev):
    rows, head_width = q_heads.shape
    keys = k_all.shape[0]
    scale = DH ** (-0.5)
    pair = heads_at_once(heads_dev)
    wide = pair * DH
    step = math.gcd(rows, 256)

    def kernel(q_ref, k_ref, v_ref, out_ref, lse_ref):
        for block in range(rows // step):
            here_rows = slice(block * step, (block + 1) * step)
            sums = []
            for h in range(pair):
                cols = slice(h * DH, (h + 1) * DH)
                scores = contract(k_ref[:, cols], q_ref[here_rows, cols], (1, 1)) * scale
                best = jnp.max(scores, axis=0, keepdims=True)
                weights = jnp.exp(scores - best)
                total = jnp.sum(weights, axis=0, keepdims=True)
                accum = contract(v_ref[:, cols], weights.astype(jnp.bfloat16), (0, 0))
                sums.append(accum / total)
                lse_ref[0, h : h + 1, here_rows] = best + jnp.log(total)
            out_ref[here_rows, :] = jnp.concatenate(sums, axis=0).T.astype(jnp.bfloat16)

    return pl.pallas_call(
        kernel,
        name="attend_forward",
        grid=(heads_dev // pair,),
        in_specs=[
            pl.BlockSpec((rows, wide), lambda g: (0, g)),
            pl.BlockSpec((keys, wide), lambda g: (0, g)),
            pl.BlockSpec((keys, wide), lambda g: (0, g)),
        ],
        out_specs=[
            pl.BlockSpec((rows, wide), lambda g: (0, g)),
            pl.BlockSpec((1, pair, rows), lambda g: (g, 0, 0)),
        ],
        out_shape=[
            jax.ShapeDtypeStruct((rows, head_width), jnp.bfloat16),
            jax.ShapeDtypeStruct((heads_dev // pair, pair, rows), jnp.float32),
        ],
    )(q_heads, k_all, v_all)


def attend_backward(q_heads, k_all, v_all, attended, lse, d_att, heads_dev):
    rows, head_width = q_heads.shape
    keys = k_all.shape[0]
    scale = DH ** (-0.5)
    pair = heads_at_once(heads_dev)
    wide = pair * DH
    size = math.gcd(keys, 512)
    steps = keys // size

    def kernel(q_ref, k_ref, v_ref, att_ref, lse_ref, d_ref, dq_ref, dk_ref, dv_ref, accum, delta):
        step = pl.program_id(1)

        @pl.when(step == 0)
        def unused_start():
            accum[...] = jnp.zeros_like(accum)
            both = (d_ref[...].astype(jnp.float32) * att_ref[...].astype(jnp.float32)).T
            for h in range(pair):
                delta[h : h + 1, :] = jnp.sum(both[h * DH : (h + 1) * DH], axis=0, keepdims=True)

        for h in range(pair):
            cols = slice(h * DH, (h + 1) * DH)
            k_head, q_head, d_head = k_ref[:, cols], q_ref[:, cols], d_ref[:, cols]
            scores = contract(k_head, q_head, (1, 1)) * scale
            weights = jnp.exp(scores - lse_ref[0, h : h + 1, :])
            d_weights = contract(v_ref[:, cols], d_head, (1, 1))
            d_scores = (weights * (d_weights - delta[h : h + 1, :])).astype(jnp.bfloat16)
            dv_ref[:, cols] = contract(weights.astype(jnp.bfloat16), d_head, (1, 0)).astype(jnp.bfloat16)
            dk_ref[:, cols] = (contract(d_scores, q_head, (1, 0)) * scale).astype(jnp.bfloat16)
            accum[cols, :] += contract(k_head, d_scores, (0, 0))

        @pl.when(step == steps - 1)
        def unused_end():
            dq_ref[...] = (accum[...] * scale).T.astype(jnp.bfloat16)

    across = pl.BlockSpec((rows, wide), lambda g, s: (0, g))
    down = pl.BlockSpec((size, wide), lambda g, s: (s, g))
    return pl.pallas_call(
        kernel,
        name="attend_backward",
        grid=(heads_dev // pair, steps),
        in_specs=[
            across,
            down,
            down,
            across,
            pl.BlockSpec((1, pair, rows), lambda g, s: (g, 0, 0)),
            across,
        ],
        out_specs=[across, down, down],
        out_shape=[
            jax.ShapeDtypeStruct((rows, head_width), jnp.bfloat16),
            jax.ShapeDtypeStruct((keys, head_width), jnp.bfloat16),
            jax.ShapeDtypeStruct((keys, head_width), jnp.bfloat16),
        ],
        scratch_shapes=[pltpu.VMEM((wide, rows), jnp.float32), pltpu.VMEM((pair, rows), jnp.float32)],
    )(q_heads, k_all, v_all, attended, lse, d_att)


def local(
    tokens,
    query_weight,
    key_weight,
    value_weight,
    out_weight,
    query_bias,
    value_bias,
    out_bias,
    norm1_gain,
    norm1_shift,
    inner_weight,
    inner_bias,
    outer_weight,
    outer_bias,
    norm2_gain,
    norm2_shift,
    out_grad,
):
    group = ("dp", "blk")
    slots = lax.axis_size("dp") * lax.axis_size("blk")
    blocks = lax.axis_size("blk")
    lanes = lax.axis_size("ulysses")
    rows_in = tokens[0]
    tok_rows, width = rows_in.shape
    head_width = query_weight.shape[1]
    heads_dev = head_width // DH
    inner_width = inner_weight.shape[1]
    small_in = (
        out_bias,
        norm1_gain,
        norm1_shift,
        outer_bias,
        norm2_gain,
        norm2_shift,
        query_bias,
        value_bias,
        inner_bias,
    )
    (tok_all,), (q3, k3, v3, o3, small) = communicate(
        0,
        [
            LineGather([rows_in]),
            CubeGather(
                group,
                [
                    query_weight,
                    key_weight,
                    value_weight,
                    out_weight,
                    pack([a.reshape(1, -1) for a in small_in], 1)[0],
                ],
                (False, False, False, True, False),
            ),
        ],
    )
    rows_all = tok_all.reshape(-1, width)
    w_query, w_key, w_value = (w.reshape(width, head_width) for w in (q3, k3, v3))
    w_out = join_columns(o3)
    flat = small.reshape(slots, -1)
    vectors = []
    start = 0
    for a in small_in:
        piece = flat[:, start : start + a.size]
        start += a.size
        if a.ndim == 2:
            piece = piece.reshape((slots,) + a.shape).transpose(1, 0, 2)
        vectors.append(piece.reshape(-1))
    b_out, gain_one, shift_one, b_outer, gain_two, shift_two, b_query, b_value, b_inner = vectors
    q_heads = (mat(rows_all, w_query) + b_query).astype(jnp.bfloat16)
    k_heads = mat(rows_all, w_key).astype(jnp.bfloat16)
    v_heads = (mat(rows_all, w_value) + b_value).astype(jnp.bfloat16)
    k_all, v_all = communicate(1, [CubeGather(("blk",), [k_heads, v_heads])])[0]
    k_all = k_all.reshape(-1, head_width)
    v_all = v_all.reshape(-1, head_width)
    attended, lse = attend_forward(q_heads, k_all, v_all, heads_dev)
    (attn_sum,), (inner3, outer3) = communicate(
        2,
        [
            LineScatter([mat(attended, w_out).astype(jnp.bfloat16).reshape(lanes, tok_rows, width)]),
            CubeGather(group, [inner_weight, outer_weight], (False, True)),
        ],
    )
    w_inner = inner3.reshape(width, inner_width)
    w_outer = join_columns(outer3)
    resid_one = rows_in.astype(jnp.float32) + attn_sum + b_out
    normed_one, unit_one, rstd_one = norm_forward(
        resid_one, gain_one, shift_one
    )
    normed_round = normed_one.astype(jnp.bfloat16)
    normed_all = communicate(3, [LineGather([normed_round])])[0][0].reshape(-1, width)
    pre_act = mat(normed_all, w_inner) + b_inner
    act_full, slope = gelu_parts(pre_act)
    activation = act_full.astype(jnp.bfloat16)
    ffn_term = mat(activation, w_outer).astype(jnp.bfloat16).reshape(lanes, tok_rows, width)
    ffn_sum = communicate(4, [LineScatter([ffn_term])])[0][0]
    resid_two = normed_one + ffn_sum + b_outer
    final, unit_two, rstd_two = norm_forward(
        resid_two, gain_two, shift_two
    )
    block_out = final.astype(jnp.bfloat16)[None]
    d_resid_two, g_gain_two, g_shift_two = norm_backward(
        out_grad[0].astype(jnp.float32), unit_two, rstd_two, gain_two
    )
    g_outer_b = jnp.sum(d_resid_two, axis=0)
    d_two_round = d_resid_two.astype(jnp.bfloat16)
    d_two_all = communicate(5, [LineGather([d_two_round])])[0][0].reshape(-1, width)
    g_outer_w = jnp.einsum("tf,td->fd", activation, d_two_all, preferred_element_type=jnp.float32)
    d_pre = jnp.einsum("td,fd->tf", d_two_all, w_outer, preferred_element_type=jnp.float32) * slope
    d_pre_round = d_pre.astype(jnp.bfloat16)
    g_inner_w = jnp.einsum("td,tf->df", normed_all, d_pre_round, preferred_element_type=jnp.float32)
    g_inner_b = jnp.sum(d_pre, axis=0).reshape(-1, DH)
    extras_two = spread_rows([g_gain_two, g_shift_two, g_outer_b], lanes)
    d_term = jnp.einsum("tf,df->td", d_pre_round, w_inner, preferred_element_type=jnp.float32)
    (d_sum, sums_two), (r_outer,) = communicate(
        6,
        [
            LineScatter([d_term.astype(jnp.bfloat16).reshape(lanes, tok_rows, width), extras_two]),
            CubeScatter(group, [column_slots(g_outer_w, slots)]),
        ],
    )
    d_normed = d_resid_two + d_sum
    d_resid_one, g_gain_one, g_shift_one = norm_backward(
        d_normed, unit_one, rstd_one, gain_one
    )
    g_out_b = jnp.sum(d_resid_one, axis=0)
    d_one_round = d_resid_one.astype(jnp.bfloat16)
    (d_one_all,), (r_inner,) = communicate(
        7,
        [LineGather([d_one_round]), CubeScatter(group, [row_slots(g_inner_w, slots)])],
    )
    d_one_all = d_one_all.reshape(-1, width)
    g_out_w = jnp.einsum("te,td->ed", attended, d_one_all, preferred_element_type=jnp.float32)
    d_att = jnp.einsum("td,ed->te", d_one_all, w_out, preferred_element_type=jnp.float32).astype(
        jnp.bfloat16
    )
    dq_heads, k_terms, v_terms = attend_backward(
        q_heads, k_all, v_all, attended, lse, d_att, heads_dev
    )
    extras_one = spread_rows([g_gain_one, g_shift_one, g_out_b], lanes)
    (sums_one,), owned = communicate(
        8,
        [
            LineScatter([extras_one]),
            CubeScatter(("blk",), [part.reshape(blocks, -1, head_width) for part in (k_terms, v_terms)]),
        ],
    )
    dk_heads, dv_heads = (part.astype(jnp.bfloat16) for part in owned)
    g_query_w = jnp.einsum("td,te->de", rows_all, dq_heads, preferred_element_type=jnp.float32)
    g_key_w = jnp.einsum("td,te->de", rows_all, dk_heads, preferred_element_type=jnp.float32)
    g_value_w = jnp.einsum("td,te->de", rows_all, dv_heads, preferred_element_type=jnp.float32)
    g_query_b = jnp.sum(dq_heads.astype(jnp.float32), axis=0).reshape(-1, DH)
    g_value_b = jnp.sum(dv_heads.astype(jnp.float32), axis=0).reshape(-1, DH)
    small_out = [v.reshape(slots, -1) for v in (*sums_one[:3], *sums_two[:3])]
    for bias in (g_query_b, g_value_b, g_inner_b):
        count = bias.shape[0]
        small_out.append(bias.reshape(count, slots, -1).transpose(1, 0, 2).reshape(slots, -1))
    back = None
    for grad, weight in ((dq_heads, w_query), (dk_heads, w_key), (dv_heads, w_value)):
        term = jnp.einsum("te,de->td", grad, weight, preferred_element_type=jnp.float32)
        back = term if back is None else back + term
    (back_sum,), (r_query, r_key, r_value, r_out, kept) = communicate(
        9,
        [
            LineScatter([back.astype(jnp.bfloat16).reshape(lanes, tok_rows, width)]),
            CubeScatter(
                group,
                [
                    row_slots(g_query_w, slots),
                    row_slots(g_key_w, slots),
                    row_slots(g_value_w, slots),
                    column_slots(g_out_w, slots),
                    pack(small_out, slots),
                ],
            ),
        ],
    )
    tokens_grad = (d_resid_one + back_sum).astype(jnp.bfloat16)[None]
    kept = kept.reshape(-1)
    ends = []
    start = 0
    for piece in small_out:
        ends.append(kept[start : start + piece.shape[1]])
        start += piece.shape[1]
    gain1, shift1, outb, gain2, shift2, outerb, queryb, valueb, innerb = ends
    return (
        block_out,
        tokens_grad,
        r_query,
        r_key,
        r_value,
        r_out,
        queryb.reshape(query_bias.shape),
        valueb.reshape(value_bias.shape),
        outb,
        gain1,
        shift1,
        r_inner,
        innerb.reshape(inner_bias.shape),
        r_outer,
        outerb,
        gain2,
        shift2,
    )


def solution(mesh):
    in_specs = (
        P("dp", ("blk", "ulysses"), None),
        P(("dp", "blk"), "ulysses"),
        P(("dp", "blk"), "ulysses"),
        P(("dp", "blk"), "ulysses"),
        P("ulysses", ("dp", "blk")),
        P("ulysses", ("dp", "blk")),
        P("ulysses", ("dp", "blk")),
        P(("dp", "blk")),
        P(("dp", "blk")),
        P(("dp", "blk")),
        P(("dp", "blk"), "ulysses"),
        P("ulysses", ("dp", "blk")),
        P("ulysses", ("dp", "blk")),
        P(("dp", "blk")),
        P(("dp", "blk")),
        P(("dp", "blk")),
        P("dp", ("blk", "ulysses"), None),
    )
    out_specs = (
        P("dp", ("blk", "ulysses"), None),
        P("dp", ("blk", "ulysses"), None),
        P(("dp", "blk"), "ulysses"),
        P(("dp", "blk"), "ulysses"),
        P(("dp", "blk"), "ulysses"),
        P("ulysses", ("dp", "blk")),
        P("ulysses", ("dp", "blk")),
        P("ulysses", ("dp", "blk")),
        P(("dp", "blk")),
        P(("dp", "blk")),
        P(("dp", "blk")),
        P(("dp", "blk"), "ulysses"),
        P("ulysses", ("dp", "blk")),
        P("ulysses", ("dp", "blk")),
        P(("dp", "blk")),
        P(("dp", "blk")),
        P(("dp", "blk")),
    )
    return jax.shard_map(local, mesh=mesh, in_specs=in_specs, out_specs=out_specs, check_vma=False)
```

```python
import math

import jax
import jax.numpy as jnp
from jax import lax
from jax.experimental import pallas as pl
from jax.experimental.pallas import tpu as pltpu
from jax.sharding import PartitionSpec as P

DH = 64


EPSILON = 1e-05


def gelu_parts(pre):
    cdf = 0.5 * (1.0 + lax.erf(pre * 0.7071067811865476))
    dens = jnp.exp(-0.5 * pre * pre) * 0.3989422804014327
    return (pre * cdf, cdf + pre * dens)


def norm_forward(resid, gain, shift):
    centre = resid - jnp.mean(resid, axis=-1, keepdims=True)
    rstd = lax.rsqrt(jnp.mean(centre * centre, axis=-1, keepdims=True) + EPSILON)
    unit = centre * rstd
    return (unit * gain + shift, unit, rstd)


def norm_backward(grad, unit, rstd, gain):
    scaled = grad * gain
    inner = (
        scaled
        - jnp.mean(scaled, axis=-1, keepdims=True)
        - unit * jnp.mean(scaled * unit, axis=-1, keepdims=True)
    )
    return (rstd * inner, jnp.sum(grad * unit, axis=0), jnp.sum(grad, axis=0))


def mat(left, right):
    return jnp.dot(left, right, preferred_element_type=jnp.float32)


MESH = pl.DeviceIdType.MESH
ORDER = ("dp", "blk", "ulysses")


def here():
    return {name: lax.axis_index(name) for name in ORDER}


def bits_of(axes):
    bits = []
    below = 1
    for name in reversed(axes):
        size = lax.axis_size(name)
        stride = 1
        while stride < size:
            bits.append((name, stride, stride * below))
            stride *= 2
        below *= size
    return bits


def slot_of(axes, at):
    index = 0
    for name in axes:
        index = index * lax.axis_size(name) + at[name]
    return index


def flip(index, stride):
    return index + stride * (1 - 2 * ((index // stride) % 2))


def flip_all(index, bits):
    for bit in bits:
        index = flip(index, bit[2])
    return index


def peer(at, bit):
    name, stride, unused = bit
    return tuple(flip(at[axis], stride) if axis == name else at[axis] for axis in ORDER)


def subsets(bits):
    found = [()]
    for bit in bits:
        found = found + [sub + (bit,) for sub in found]
    return found


def row_parts(rows, size, tile):
    if size < 65536 or rows % (2 * tile):
        return [(0, rows)]
    return [(0, rows // 2), (rows // 2, rows // 2)]


def row_loop(rows, body):
    step = math.gcd(rows, 64)

    def turn(i, carry):
        body(pl.ds(pl.multiple_of(i * step, step), step))
        return carry

    lax.fori_loop(0, rows // step, turn, 0)


class Sems:
    def __init__(self, ref=None):
        self.ref, self.count = ref, 0

    def take(self):
        self.count += 1
        return self.count - 1 if self.ref is None else self.ref.at[self.count - 1]


def remote(src, dst, sems, to):
    return pltpu.make_async_remote_copy(
        src_ref=src, dst_ref=dst, send_sem=sems[0], recv_sem=sems[1], device_id=to, device_id_type=MESH
    )


def slab(slot, width):
    return pl.ds(pl.multiple_of(slot * width, width), width)


def slot_rows(ref, slot, rows, width):
    return ref.at[slot, rows] if len(ref.shape) == 3 else ref.at[rows, slab(slot, width)]


class CubeGather:
    def __init__(self, axes, arrays, columns=(False,) * 8):
        self.axes, self.arrays, self.bits = axes, list(arrays), bits_of(axes)
        self.slots = math.prod(lax.axis_size(name) for name in axes)
        self.flat = [joined and a.shape[1] % 128 == 0 for a, joined in zip(self.arrays, columns)]
        self.outs = [
            jax.ShapeDtypeStruct(
                (a.shape[0], self.slots * a.shape[1]) if flat else (self.slots,) + a.shape, a.dtype
            )
            for a, flat in zip(self.arrays, self.flat)
        ]
        self.scratch = []
        streams = sum(len(self.parts(a)) for a in self.arrays)
        self.sems = 2 * streams * (self.slots - 1)

    def parts(self, array):
        return row_parts(array.shape[0], array.size, 16)

    def peers(self, at):
        return [(peer(at, bit), None) for bit in self.bits]

    def run(self, at, ins, outs, scratch, sems):
        gens = []
        me = slot_of(self.axes, at)
        for array, src, dst in zip(self.arrays, ins, outs):
            for number, part in enumerate(self.parts(array)):
                far = self.bits[1:]
                order = (far if number else far[::-1]) + self.bits[:1]
                gens.append(self.stream(at, me, src, dst, part, order, sems))
        yield from together(gens)
        for src, dst in zip(ins, outs):
            if len(dst.shape) == 2:
                dst[:, slab(me, src.shape[1])] = src[...]
            else:
                dst[me] = src[...]

    def stream(self, at, me, src, dst, part, order, sems):
        rows = pl.ds(*part)
        held, landing, sent = [()], {}, []
        for bit in order:
            fresh = {}
            for sub in held:
                if sub in landing:
                    landing.pop(sub).wait_recv()
                slot = flip_all(me, sub)
                there = slot_rows(dst, slot, rows, src.shape[1])
                copy = remote(
                    there if sub else src.at[rows], there, (sems.take(), sems.take()), peer(at, bit)
                )
                copy.start()
                sent.append(copy)
                fresh[sub + (bit,)] = copy
            landing.update(fresh)
            held = held + list(fresh)
            yield
        for copy in landing.values():
            copy.wait_recv()
        for copy in sent:
            copy.wait_send()


class CubeScatter:
    def __init__(self, axes, arrays):
        self.axes, self.arrays, self.bits = axes, list(arrays), bits_of(axes)
        self.slots = math.prod(lax.axis_size(name) for name in axes)
        self.outs = [jax.ShapeDtypeStruct(self.piece(a), jnp.float32) for a in self.arrays]
        self.scratch = []
        self.sems = 0
        for a in self.arrays:
            width = self.piece(a)[1]
            for part in self.parts(a):
                left = self.slots
                for unused in self.bits:
                    left //= 2
                    self.scratch.append(((left, part[1], width), a.dtype))
                    if left > 1:
                        self.scratch.append(((left, part[1], width), a.dtype))
                self.sems += 2 * (self.slots - 1)

    def piece(self, array):
        return array.shape[1:] if array.ndim == 3 else (array.shape[0], array.shape[1] // self.slots)

    def parts(self, array):
        return row_parts(self.piece(array)[0], array.size // self.slots, 16)

    def peers(self, at):
        return [(peer(at, bit), None) for bit in self.bits]

    def run(self, at, ins, outs, scratch, sems):
        gens = []
        me = slot_of(self.axes, at)
        scratch = list(scratch)
        for array, src, dst in zip(self.arrays, ins, outs):
            for number, part in enumerate(self.parts(array)):
                far = self.bits[1:]
                order = self.bits[:1] + (far if number else far[::-1])
                own = scratch[: 2 * len(order) - 1]
                scratch = scratch[2 * len(order) - 1 :]
                gens.append(self.stream(at, me, src, dst, part, order, own, sems))
        yield from together(gens)

    def stream(self, at, me, src, dst, part, order, scratch, sems):
        start, count = part
        rows = pl.ds(start, count)
        level = None
        sent = []
        for stage, bit in enumerate(order):
            rest = order[stage + 1 :]
            subs = subsets(rest)
            before = subsets(order[stage:])
            landed = scratch[2 * stage]
            copies = []
            for j, sub in enumerate(subs):
                if level is None:
                    piece = slot_rows(src, flip_all(flip(me, bit[2]), sub), rows, dst.shape[1])
                else:
                    piece = level.at[before.index((bit,) + sub)]
                copy = remote(piece, landed.at[j], (sems.take(), sems.take()), peer(at, bit))
                copy.start()
                copies.append(copy)
            sent += copies
            yield
            goal = None if not rest else scratch[2 * stage + 1]
            for j, sub in enumerate(subs):
                copies[j].wait_recv()
                slot = None if level is not None else flip_all(me, sub)
                old = None if level is None else before.index(sub)

                def add(here_rows, j=j, slot=slot, old=old, level=level, goal=goal, landed=landed):
                    moved = pl.ds(start + here_rows.start, here_rows.size)
                    if level is not None:
                        mine = level[old, here_rows, :]
                    elif len(src.shape) == 3:
                        mine = src[slot, moved, :]
                    else:
                        mine = src[moved, slab(slot, dst.shape[1])]
                    total = mine.astype(jnp.float32) + landed[j, here_rows, :].astype(jnp.float32)
                    if goal is None:
                        dst[moved, :] = total
                    else:
                        goal[j, here_rows, :] = total.astype(goal.dtype)

                row_loop(count, add)
            level = goal
        for copy in sent:
            copy.wait_send()


def line_peers(at, size):
    spot = at["ulysses"]
    return [
        ((at["dp"], at["blk"], spot + 1), spot < size - 1),
        ((at["dp"], at["blk"], spot - 1), spot > 0),
    ]


class LineGather:
    def __init__(self, arrays):
        self.arrays, self.size = list(arrays), lax.axis_size("ulysses")
        self.outs = [jax.ShapeDtypeStruct((self.size,) + a.shape, a.dtype) for a in self.arrays]
        self.scratch = []
        streams = sum(len(self.parts(a)) for a in self.arrays)
        self.sems = streams * 4 * (self.size - 1)

    def parts(self, array):
        return row_parts(array.shape[0], array.size, 16)

    def peers(self, at):
        return line_peers(at, self.size)

    def run(self, at, ins, outs, scratch, sems):
        gens = [
            self.stream(at, src, dst, part, sems)
            for array, src, dst in zip(self.arrays, ins, outs)
            for part in self.parts(array)
        ]
        yield from together(gens)
        for src, dst in zip(ins, outs):
            dst[at["ulysses"]] = src[...]

    def stream(self, at, src, dst, part, sems):
        size, spot = self.size, at["ulysses"]
        rows = pl.ds(*part)
        ways = []
        for sign in (1, -1):
            tail = spot if sign > 0 else size - 1 - spot
            to = (at["dp"], at["blk"], spot + sign)
            pairs = [(sems.take(), sems.take()) for unused in range(size - 1)]
            ways.append((sign, tail, to, pairs))

        def copy(way, step):
            sign, tail, to, pairs = way
            slot = spot - sign * step
            there = dst.at[slot, rows]
            return remote(src.at[rows] if step == 0 else there, there, pairs[step], to)

        for step in range(size):
            for way in ways:
                tail = way[1]
                if step > 0:

                    @pl.when(tail >= step)
                    def unused_wait(way=way, step=step):
                        copy(way, step - 1).wait_recv()

                if step < size - 1:

                    @pl.when(jnp.logical_and(tail < size - 1, tail >= step))
                    def unused_send(way=way, step=step):
                        copy(way, step).start()

            yield
        for way in ways:
            for step in range(size - 1):

                @pl.when(jnp.logical_and(way[1] < size - 1, way[1] >= step))
                def unused_sent(way=way, step=step):
                    copy(way, step).wait_send()


class LineScatter:
    def __init__(self, arrays):
        self.arrays, self.size = list(arrays), lax.axis_size("ulysses")
        self.outs = [jax.ShapeDtypeStruct(a.shape[1:], jnp.float32) for a in self.arrays]
        self.scratch = []
        self.sems = 0
        for a in self.arrays:
            for part in self.parts(a):
                shape = (2, 2, self.size - 1, part[1], a.shape[2])
                self.scratch.append((shape, a.dtype))
                self.sems += 4 * (self.size - 1)

    def parts(self, array):
        return row_parts(array.shape[1], array.size // self.size, 16)

    def peers(self, at):
        return line_peers(at, self.size)

    def run(self, at, ins, outs, scratch, sems):
        gens, scratch = [], list(scratch)
        for array, src, dst in zip(self.arrays, ins, outs):
            for part in self.parts(array):
                gens.append(self.stream(at, src, dst, part, scratch.pop(0), sems))
        yield from together(gens)

    def stream(self, at, src, dst, part, room, sems):
        size, spot = self.size, at["ulysses"]
        start, count = part
        ways = []
        for index, sign in enumerate((1, -1)):
            tail = spot if sign > 0 else size - 1 - spot
            to = (at["dp"], at["blk"], spot + sign)
            pairs = [(sems.take(), sems.take()) for unused in range(size - 1)]
            ways.append((index, sign, tail, to, pairs))

        def owner(way, step):
            return spot + way[1] * (size - 1 - step)

        def copy(way, step, first):
            index, sign, tail, to, pairs = way
            piece = src.at[owner(way, step), pl.ds(start, count)] if first else room.at[index, 1, step]
            return remote(piece, room.at[index, 0, step], pairs[step], to)

        for step in range(size - 1):
            for way in ways:

                @pl.when(way[2] == 0)
                def unused_first(way=way, step=step):
                    copy(way, step, True).start()

                if step > 0:

                    @pl.when(jnp.logical_and(way[2] >= 1, way[2] <= step))
                    def unused_next(way=way, step=step):
                        index = way[0]
                        copy(way, step - 1, False).wait_recv()

                        def add(rows):
                            moved = pl.ds(start + rows.start, rows.size)
                            total = src[owner(way, step), moved, :].astype(jnp.float32) + room[
                                index, 0, step - 1, rows, :
                            ].astype(jnp.float32)
                            room[index, 1, step, rows, :] = total.astype(room.dtype)

                        row_loop(count, add)
                        copy(way, step, False).start()

            yield

        def begin(rows):
            moved = pl.ds(start + rows.start, rows.size)
            dst[moved, :] = src[spot, moved, :].astype(jnp.float32)

        row_loop(count, begin)
        for way in ways:

            @pl.when(way[2] >= 1)
            def unused_last(way=way):
                copy(way, size - 2, False).wait_recv()

                def add(rows):
                    moved = pl.ds(start + rows.start, rows.size)
                    dst[moved, :] = dst[moved, :] + room[way[0], 0, size - 2, rows, :].astype(jnp.float32)

                row_loop(count, add)

        for way in ways:
            for step in range(size - 1):

                @pl.when(way[2] == 0)
                def unused_sent_first(way=way, step=step):
                    copy(way, step, True).wait_send()

                if step > 0:

                    @pl.when(jnp.logical_and(way[2] >= 1, way[2] <= step))
                    def unused_sent(way=way, step=step):
                        copy(way, step, False).wait_send()


def together(gens):
    gens = list(gens)
    while gens:
        alive = []
        for gen in gens:
            try:
                next(gen)
                alive.append(gen)
            except StopIteration:
                pass
        gens = alive
        if gens:
            yield


def communicate(number, tasks):
    arrays = [a for task in tasks for a in task.arrays]
    outs = [o for task in tasks for o in task.outs]
    rooms = [s for task in tasks for s in task.scratch]
    count = sum(task.sems for task in tasks)

    def kernel(*refs):
        ins, refs = refs[: len(arrays)], refs[len(arrays) :]
        results, refs = refs[: len(outs)], refs[len(outs) :]
        scratch, sem_ref = refs[: len(rooms)], refs[len(rooms)]
        at = here()
        barrier = pltpu.get_barrier_semaphore()
        total = 0
        seen = set()
        for task in tasks:
            kind = type(task) in (LineGather, LineScatter)
            for place, (to, exists) in enumerate(task.peers(at)):
                name = ("line", place) if kind else task.bits[place][:2]
                if name in seen:
                    continue
                seen.add(name)
                if exists is None:
                    pl.semaphore_signal(barrier, inc=1, device_id=to, device_id_type=MESH)
                    total = total + 1
                else:

                    @pl.when(exists)
                    def unused_greet(to=to):
                        pl.semaphore_signal(barrier, inc=1, device_id=to, device_id_type=MESH)

                    total = total + exists.astype(jnp.int32)
        pl.semaphore_wait(barrier, total)
        sems = Sems(sem_ref)
        gens = []
        for task in tasks:
            n_in, n_out, n_room = len(task.arrays), len(task.outs), len(task.scratch)
            gens.append(task.run(at, ins[:n_in], results[:n_out], scratch[:n_room], sems))
            ins, results, scratch = ins[n_in:], results[n_out:], scratch[n_room:]
        for unused in together(gens):
            pass

    flat = pl.pallas_call(
        kernel,
        name="exchange_%d" % number,
        out_shape=outs,
        in_specs=[pl.BlockSpec(memory_space=pltpu.VMEM)] * len(arrays),
        out_specs=[pl.BlockSpec(memory_space=pltpu.VMEM)] * len(outs),
        scratch_shapes=[pltpu.VMEM(*room) for room in rooms] + [pltpu.SemaphoreType.DMA((count,))],
        compiler_params=pltpu.CompilerParams(collective_id=number, has_side_effects=True),
    )(*arrays)
    flat = list(flat)
    split = []
    for task in tasks:
        split.append(flat[: len(task.outs)])
        flat = flat[len(task.outs) :]
    return split


def pack(pieces, slots):
    joined = jnp.concatenate([p.astype(jnp.float32) for p in pieces], axis=1)
    length = joined.shape[1]
    padded = -(-length // 1024) * 1024
    return jnp.pad(joined, ((0, 0), (0, padded - length))).reshape(slots, padded // 128, 128)


def row_slots(grad, slots):
    return grad.astype(jnp.bfloat16).reshape(slots, -1, grad.shape[1])


def column_slots(grad, slots):
    if grad.shape[1] % (128 * slots) == 0:
        return grad.astype(jnp.bfloat16)
    return grad.astype(jnp.bfloat16).reshape(grad.shape[0], slots, -1).transpose(1, 0, 2)


def join_columns(gathered):
    if gathered.ndim == 2:
        return gathered
    return gathered.transpose(1, 0, 2).reshape(gathered.shape[1], -1)


def spread_rows(vectors, lanes):
    rows = jnp.pad(jnp.stack(vectors), ((0, -len(vectors) % 8), (0, 0)))
    return jnp.broadcast_to(rows[None], (lanes,) + rows.shape)


def contract(left, right, sides):
    return lax.dot_general(left, right, ((sides[:1], sides[1:]), ((), ())), preferred_element_type=jnp.float32)


def greet(at, bits):
    barrier = pltpu.get_barrier_semaphore()
    for bit in bits:
        pl.semaphore_signal(barrier, inc=1, device_id=peer(at, bit), device_id_type=MESH)
    pl.semaphore_wait(barrier, len(bits))


def attend_forward(q_heads, k_heads, v_heads, heads_dev):
    rows, head_width = q_heads.shape
    scale = DH ** (-0.5)
    bits = bits_of(("blk",))
    blocks = lax.axis_size("blk")
    order = bits[1:] + bits[:1]
    subs = sorted(subsets(order)[1:], key=lambda sub: (sub != tuple(bits[:1]), len(sub)))
    step = math.gcd(rows, 256)

    def kernel(q_ref, k_ref, v_ref, k_all, v_all, out_ref, lse_ref, best, total, accum, sem_ref):
        at = here()
        me = at["blk"]
        greet(at, bits)
        sems = Sems(sem_ref)
        landing, sent = {}, []

        def pass_on(sub):
            first = order.index(sub[-1]) + 1 if sub else 0
            slot = flip_all(me, sub)
            for bit in order[first:]:
                copies = []
                for src, dst in ((k_ref, k_all), (v_ref, v_all)):
                    piece = dst.at[slot] if sub else src
                    copies.append(
                        remote(piece, dst.at[slot], (sems.take(), sems.take()), peer(at, bit))
                    )
                    copies[-1].start()
                landing[sub + (bit,)] = copies
                sent.extend(copies)

        def fold(k_piece, v_piece, slot):
            def turn(i, carry):
                span = pl.ds(pl.multiple_of(i * step, step), step)
                for h in range(heads_dev):
                    cols = slice(h * DH, (h + 1) * DH)
                    one = slice(h, h + 1)
                    k_head = k_piece[:, cols] if slot is None else k_piece[slot, :, cols]
                    v_head = v_piece[:, cols] if slot is None else v_piece[slot, :, cols]
                    scores = contract(k_head, q_ref[span, cols], (1, 1)) * scale
                    top = jnp.max(scores, axis=0, keepdims=True)
                    if slot is not None:
                        top = jnp.maximum(best[one, span], top)
                    weights = jnp.exp(scores - top)
                    mass = jnp.sum(weights, axis=0, keepdims=True)
                    update = contract(v_head, weights.astype(jnp.bfloat16), (0, 0))
                    if slot is not None:
                        fade = jnp.exp(best[one, span] - top)
                        mass = mass + total[one, span] * fade
                        update = update + accum[cols, span] * fade
                    best[one, span] = top
                    total[one, span] = mass
                    accum[cols, span] = update
                return carry

            lax.fori_loop(0, rows // step, turn, 0)

        pass_on(())
        fold(k_ref, v_ref, None)
        for sub in subs:
            for copy in landing[sub]:
                copy.wait_recv()
            pass_on(sub)
            fold(k_all, v_all, flip_all(me, sub))
        k_all[me] = k_ref[...]
        v_all[me] = v_ref[...]
        lse_ref[...] = best[...] + jnp.log(total[...])
        for h in range(heads_dev):
            cols = slice(h * DH, (h + 1) * DH)
            accum[cols, :] = accum[cols, :] / total[h : h + 1, :]
        out_ref[...] = accum[...].T.astype(jnp.bfloat16)
        for copy in sent:
            copy.wait_send()

    vmem = pl.BlockSpec(memory_space=pltpu.VMEM)
    whole = jax.ShapeDtypeStruct((blocks, rows, head_width), jnp.bfloat16)
    return pl.pallas_call(
        kernel,
        name="attend_forward",
        in_specs=[vmem] * 3,
        out_specs=[vmem] * 4,
        out_shape=[
            whole,
            whole,
            jax.ShapeDtypeStruct((rows, head_width), jnp.bfloat16),
            jax.ShapeDtypeStruct((heads_dev, rows), jnp.float32),
        ],
        scratch_shapes=[
            pltpu.VMEM((heads_dev, rows), jnp.float32),
            pltpu.VMEM((heads_dev, rows), jnp.float32),
            pltpu.VMEM((head_width, rows), jnp.float32),
            pltpu.SemaphoreType.DMA((4 * (blocks - 1),)),
        ],
        compiler_params=pltpu.CompilerParams(collective_id=1, has_side_effects=True),
    )(q_heads, k_heads, v_heads)


def attend_backward(q_heads, k_all, v_all, attended, lse, d_att, heads_dev):
    rows, head_width = q_heads.shape
    blocks = lax.axis_size("blk")
    scale = DH ** (-0.5)
    bits = bits_of(("blk",))
    core, far = tuple(bits[:1]), bits[1:]
    fars = sorted(subsets(far), key=lambda sub: [bit not in sub for bit in far])
    size = math.gcd(rows, 256)

    def kernel(
        q_ref, k_ref, v_ref, att_ref, lse_ref, d_ref, dq_ref, dk_ref, dv_ref,
        accum, delta, given, kept, landed, summed, arrived, sem_ref,
    ):
        at = here()
        me = at["blk"]
        greet(at, bits)
        sems = Sems(sem_ref)
        accum[...] = jnp.zeros_like(accum)
        both = (d_ref[...].astype(jnp.float32) * att_ref[...].astype(jnp.float32)).T
        for h in range(heads_dev):
            delta[h : h + 1, :] = jnp.sum(both[h * DH : (h + 1) * DH], axis=0, keepdims=True)

        def terms(slot, goal, index):
            def turn(i, carry):
                span = pl.ds(pl.multiple_of(i * size, size), size)
                for h in range(heads_dev):
                    cols = slice(h * DH, (h + 1) * DH)
                    one = slice(h, h + 1)
                    k_head, q_head, d_head = k_ref[slot, span, cols], q_ref[:, cols], d_ref[:, cols]
                    scores = contract(k_head, q_head, (1, 1)) * scale
                    weights = jnp.exp(scores - lse_ref[one, :])
                    d_weights = contract(v_ref[slot, span, cols], d_head, (1, 1))
                    d_scores = (weights * (d_weights - delta[one, :])).astype(jnp.bfloat16)
                    v_part = contract(weights.astype(jnp.bfloat16), d_head, (1, 0))
                    k_part = contract(d_scores, q_head, (1, 0)) * scale
                    goal[index, 0, span, cols] = k_part.astype(jnp.bfloat16)
                    goal[index, 1, span, cols] = v_part.astype(jnp.bfloat16)
                    accum[cols, :] += contract(k_head, d_scores, (0, 0))
                return carry

            lax.fori_loop(0, rows // size, turn, 0)

        sent, coming = [], {}
        for index, sub in enumerate(fars):
            terms(flip_all(me, sub + core), given, index)
            copy = remote(
                given.at[index], landed.at[index], (sems.take(), sems.take()), peer(at, core[0])
            )
            copy.start()
            sent.append(copy)
            terms(flip_all(me, sub), kept, index)
            sources = [(landed, index)]
            copy.wait_recv()
            link = None
            for bit in far:
                if bit in sub:
                    link = bit
                    break
                other = coming[(bit, sub)]
                other[0].wait_recv()
                sources.append((arrived, other[1]))

            def add(span, index=index, sources=sources, link=link):
                for which, result in ((0, dk_ref), (1, dv_ref)):
                    value = kept[index, which, span, :].astype(jnp.float32)
                    for ref, place in sources:
                        value = value + ref[place, which, span, :].astype(jnp.float32)
                    if link is None:
                        result[span, :] = value.astype(jnp.bfloat16)
                    else:
                        summed[index, which, span, :] = value.astype(jnp.bfloat16)

            row_loop(rows, add)
            if link is not None:
                copy = remote(
                    summed.at[index], arrived.at[index], (sems.take(), sems.take()), peer(at, link)
                )
                copy.start()
                sent.append(copy)
                coming[(link, tuple(bit for bit in sub if bit != link))] = (copy, index)
        dq_ref[...] = (accum[...] * scale).T.astype(jnp.bfloat16)
        for copy in sent:
            copy.wait_send()

    vmem = pl.BlockSpec(memory_space=pltpu.VMEM)
    out = jax.ShapeDtypeStruct((rows, head_width), jnp.bfloat16)
    room = pltpu.VMEM((len(fars), 2, rows, head_width), jnp.bfloat16)
    return pl.pallas_call(
        kernel,
        name="attend_backward",
        in_specs=[vmem] * 6,
        out_specs=[vmem] * 3,
        out_shape=[out, out, out],
        scratch_shapes=[
            pltpu.VMEM((head_width, rows), jnp.float32),
            pltpu.VMEM((heads_dev, rows), jnp.float32),
            room,
            room,
            room,
            room,
            room,
            pltpu.SemaphoreType.DMA((4 * len(fars) - 2,)),
        ],
        compiler_params=pltpu.CompilerParams(collective_id=8, has_side_effects=True),
    )(q_heads, k_all, v_all, attended, lse, d_att)


def local(
    tokens,
    query_weight,
    key_weight,
    value_weight,
    out_weight,
    query_bias,
    value_bias,
    out_bias,
    norm1_gain,
    norm1_shift,
    inner_weight,
    inner_bias,
    outer_weight,
    outer_bias,
    norm2_gain,
    norm2_shift,
    out_grad,
):
    group = ("dp", "blk")
    slots = lax.axis_size("dp") * lax.axis_size("blk")
    lanes = lax.axis_size("ulysses")
    rows_in = tokens[0]
    tok_rows, width = rows_in.shape
    head_width = query_weight.shape[1]
    heads_dev = head_width // DH
    inner_width = inner_weight.shape[1]
    small_in = (
        out_bias,
        norm1_gain,
        norm1_shift,
        outer_bias,
        norm2_gain,
        norm2_shift,
        query_bias,
        value_bias,
        inner_bias,
    )
    (tok_all,), (q3, k3, v3, o3, small) = communicate(
        0,
        [
            LineGather([rows_in]),
            CubeGather(
                group,
                [
                    query_weight,
                    key_weight,
                    value_weight,
                    out_weight,
                    pack([a.reshape(1, -1) for a in small_in], 1)[0],
                ],
                (False, False, False, True, False),
            ),
        ],
    )
    rows_all = tok_all.reshape(-1, width)
    w_query, w_key, w_value = (w.reshape(width, head_width) for w in (q3, k3, v3))
    w_out = join_columns(o3)
    flat = small.reshape(slots, -1)
    vectors = []
    start = 0
    for a in small_in:
        piece = flat[:, start : start + a.size]
        start += a.size
        if a.ndim == 2:
            piece = piece.reshape((slots,) + a.shape).transpose(1, 0, 2)
        vectors.append(piece.reshape(-1))
    b_out, gain_one, shift_one, b_outer, gain_two, shift_two, b_query, b_value, b_inner = vectors
    q_heads = (mat(rows_all, w_query) + b_query).astype(jnp.bfloat16)
    k_heads = mat(rows_all, w_key).astype(jnp.bfloat16)
    v_heads = (mat(rows_all, w_value) + b_value).astype(jnp.bfloat16)
    k_all, v_all, attended, lse = attend_forward(q_heads, k_heads, v_heads, heads_dev)
    (attn_sum,), (inner3,) = communicate(
        2,
        [
            LineScatter([mat(attended, w_out).astype(jnp.bfloat16).reshape(lanes, tok_rows, width)]),
            CubeGather(group, [inner_weight]),
        ],
    )
    w_inner = inner3.reshape(width, inner_width)
    resid_one = rows_in.astype(jnp.float32) + attn_sum + b_out
    normed_one, unit_one, rstd_one = norm_forward(
        resid_one, gain_one, shift_one
    )
    normed_round = normed_one.astype(jnp.bfloat16)
    (normed_all,), (outer3,) = communicate(
        3, [LineGather([normed_round]), CubeGather(group, [outer_weight], (True,))]
    )
    normed_all = normed_all.reshape(-1, width)
    w_outer = join_columns(outer3)
    pre_act = mat(normed_all, w_inner) + b_inner
    act_full, slope = gelu_parts(pre_act)
    activation = act_full.astype(jnp.bfloat16)
    ffn_term = mat(activation, w_outer).astype(jnp.bfloat16).reshape(lanes, tok_rows, width)
    ffn_sum = communicate(4, [LineScatter([ffn_term])])[0][0]
    resid_two = normed_one + ffn_sum + b_outer
    final, unit_two, rstd_two = norm_forward(
        resid_two, gain_two, shift_two
    )
    block_out = final.astype(jnp.bfloat16)[None]
    d_resid_two, g_gain_two, g_shift_two = norm_backward(
        out_grad[0].astype(jnp.float32), unit_two, rstd_two, gain_two
    )
    g_outer_b = jnp.sum(d_resid_two, axis=0)
    d_two_round = d_resid_two.astype(jnp.bfloat16)
    d_two_all = communicate(5, [LineGather([d_two_round])])[0][0].reshape(-1, width)
    g_outer_w = jnp.einsum("tf,td->fd", activation, d_two_all, preferred_element_type=jnp.float32)
    d_pre = jnp.einsum("td,fd->tf", d_two_all, w_outer, preferred_element_type=jnp.float32) * slope
    d_pre_round = d_pre.astype(jnp.bfloat16)
    g_inner_w = jnp.einsum("td,tf->df", normed_all, d_pre_round, preferred_element_type=jnp.float32)
    g_inner_b = jnp.sum(d_pre, axis=0).reshape(-1, DH)
    extras_two = spread_rows([g_gain_two, g_shift_two, g_outer_b], lanes)
    d_term = jnp.einsum("tf,df->td", d_pre_round, w_inner, preferred_element_type=jnp.float32)
    (d_sum, sums_two), (r_outer,) = communicate(
        6,
        [
            LineScatter([d_term.astype(jnp.bfloat16).reshape(lanes, tok_rows, width), extras_two]),
            CubeScatter(group, [column_slots(g_outer_w, slots)]),
        ],
    )
    d_normed = d_resid_two + d_sum
    d_resid_one, g_gain_one, g_shift_one = norm_backward(
        d_normed, unit_one, rstd_one, gain_one
    )
    g_out_b = jnp.sum(d_resid_one, axis=0)
    d_one_round = d_resid_one.astype(jnp.bfloat16)
    extras_one = spread_rows([g_gain_one, g_shift_one, g_out_b], lanes)
    (d_one_all,), (sums_one,), (r_inner,) = communicate(
        7,
        [
            LineGather([d_one_round]),
            LineScatter([extras_one]),
            CubeScatter(group, [row_slots(g_inner_w, slots)]),
        ],
    )
    d_one_all = d_one_all.reshape(-1, width)
    g_out_w = jnp.einsum("te,td->ed", attended, d_one_all, preferred_element_type=jnp.float32)
    d_att = jnp.einsum("td,ed->te", d_one_all, w_out, preferred_element_type=jnp.float32).astype(
        jnp.bfloat16
    )
    dq_heads, dk_heads, dv_heads = attend_backward(
        q_heads, k_all, v_all, attended, lse, d_att, heads_dev
    )
    g_query_w = jnp.einsum("td,te->de", rows_all, dq_heads, preferred_element_type=jnp.float32)
    g_key_w = jnp.einsum("td,te->de", rows_all, dk_heads, preferred_element_type=jnp.float32)
    g_value_w = jnp.einsum("td,te->de", rows_all, dv_heads, preferred_element_type=jnp.float32)
    g_query_b = jnp.sum(dq_heads.astype(jnp.float32), axis=0).reshape(-1, DH)
    g_value_b = jnp.sum(dv_heads.astype(jnp.float32), axis=0).reshape(-1, DH)
    small_out = [v.reshape(slots, -1) for v in (*sums_one[:3], *sums_two[:3])]
    for bias in (g_query_b, g_value_b, g_inner_b):
        count = bias.shape[0]
        small_out.append(bias.reshape(count, slots, -1).transpose(1, 0, 2).reshape(slots, -1))
    back = None
    for grad, weight in ((dq_heads, w_query), (dk_heads, w_key), (dv_heads, w_value)):
        term = jnp.einsum("te,de->td", grad, weight, preferred_element_type=jnp.float32)
        back = term if back is None else back + term
    (back_sum,), (r_query, r_key, r_value, r_out, kept) = communicate(
        9,
        [
            LineScatter([back.astype(jnp.bfloat16).reshape(lanes, tok_rows, width)]),
            CubeScatter(
                group,
                [
                    row_slots(g_query_w, slots),
                    row_slots(g_key_w, slots),
                    row_slots(g_value_w, slots),
                    column_slots(g_out_w, slots),
                    pack(small_out, slots),
                ],
            ),
        ],
    )
    tokens_grad = (d_resid_one + back_sum).astype(jnp.bfloat16)[None]
    kept = kept.reshape(-1)
    ends = []
    start = 0
    for piece in small_out:
        ends.append(kept[start : start + piece.shape[1]])
        start += piece.shape[1]
    gain1, shift1, outb, gain2, shift2, outerb, queryb, valueb, innerb = ends
    return (
        block_out,
        tokens_grad,
        r_query,
        r_key,
        r_value,
        r_out,
        queryb.reshape(query_bias.shape),
        valueb.reshape(value_bias.shape),
        outb,
        gain1,
        shift1,
        r_inner,
        innerb.reshape(inner_bias.shape),
        r_outer,
        outerb,
        gain2,
        shift2,
    )


def solution(mesh):
    in_specs = (
        P("dp", ("blk", "ulysses"), None),
        P(("dp", "blk"), "ulysses"),
        P(("dp", "blk"), "ulysses"),
        P(("dp", "blk"), "ulysses"),
        P("ulysses", ("dp", "blk")),
        P("ulysses", ("dp", "blk")),
        P("ulysses", ("dp", "blk")),
        P(("dp", "blk")),
        P(("dp", "blk")),
        P(("dp", "blk")),
        P(("dp", "blk"), "ulysses"),
        P("ulysses", ("dp", "blk")),
        P("ulysses", ("dp", "blk")),
        P(("dp", "blk")),
        P(("dp", "blk")),
        P(("dp", "blk")),
        P("dp", ("blk", "ulysses"), None),
    )
    out_specs = (
        P("dp", ("blk", "ulysses"), None),
        P("dp", ("blk", "ulysses"), None),
        P(("dp", "blk"), "ulysses"),
        P(("dp", "blk"), "ulysses"),
        P(("dp", "blk"), "ulysses"),
        P("ulysses", ("dp", "blk")),
        P("ulysses", ("dp", "blk")),
        P("ulysses", ("dp", "blk")),
        P(("dp", "blk")),
        P(("dp", "blk")),
        P(("dp", "blk")),
        P(("dp", "blk"), "ulysses"),
        P("ulysses", ("dp", "blk")),
        P("ulysses", ("dp", "blk")),
        P(("dp", "blk")),
        P(("dp", "blk")),
        P(("dp", "blk")),
    )
    return jax.shard_map(local, mesh=mesh, in_specs=in_specs, out_specs=out_specs, check_vma=False)
```
